128 devices in a mesh: dp: 16 (over z, x), expert: 8 (over y, core).
Axes of the slice: x: 4, y: 4, z: 4, core: 2. Of those that a mesh axis runs over, the one named last changes fastest.
Arguments:
- tokens: bfloat16 [32768, 1536], P(('dp', 'expert')), may hold values from -6 to 6
- attn_gain: float32 [1536], replicated, may hold values from 0.1 to 1.9
- ffn_gain: float32 [1536], replicated, may hold values from 0.1 to 1.9
- w_query: bfloat16 [1536, 1536], replicated, may hold values from -0.15625 to 0.15625
- w_key: bfloat16 [1536, 256], replicated, may hold values from -0.15625 to 0.15625
- w_value: bfloat16 [1536, 256], replicated, may hold values from -0.15625 to 0.15625
- w_out: bfloat16 [1536, 1536], replicated, may hold values from -0.15625 to 0.15625
- key_cache: bfloat16 [384, 2048, 256], P(('dp', 'expert')), may hold values from -200 to 200
- value_cache: bfloat16 [384, 2048, 256], P(('dp', 'expert')), may hold values from -6 to 6
- req_lengths: int32 [128, 3], P(('dp', 'expert')), may hold values from 1 to 128, 256 in all within a row
- cache_lengths: int32 [128, 3], P(('dp', 'expert')), may hold values from 1024 to 2048
- expert_ids: int32 [32768, 4], P(('dp', 'expert')), may hold values from 0 to 31, all different within a row; in each aligned block of 32 rows (0 to 31, 32 to 63, ...) at most 8 rows name the same one
- route_gate: float32 [32768, 4], P(('dp', 'expert')), may hold values from 0.1 to 1
- replica_owner: int32 [32, 8], replicated, may hold values from 0 to 7, each once within a row
- replica_pick: int32 [128, 8], P(('dp', 'expert')), may hold values from 0 to 7, each once within a row
- w_gate_up: bfloat16 [32, 768, 2, 1536], P('dp', 'expert'), may hold values from -0.15625 to 0.15625
- w_down: bfloat16 [32, 1536, 768], P('dp', 'expert'), may hold values from -0.21875 to 0.21875
Outputs:
- layer_out: bfloat16 [32768, 1536], P(('dp', 'expert'))
- owner_rows: int32 [128, 2], P(('dp', 'expert'))
The draws below stay inside these ranges and needn't reach their ends.
Inputs may be any that keep to these rules, and one draw needn't show every extreme that they name: `req_lengths`: a row holds one device's request lengths in the order of its tokens; it sums to 256 and its largest is 128. `expert_ids`: a token's 4 ids differ; in each aligned block of 32 tokens no expert is named more than 8 times. `replica_owner`: each expert's row names every index of the expert axis once. `replica_pick`: each device's row names every replica once.
All inputs are finite; a program needn't handle non-finite values.
Results may differ from the reference program's by a relative error of at most 0.015.
Values may be sent and summed in bfloat16 or wider, within the bound.
A program may use at most 192 MiB of HBM per device.

```python
import math
import jax
import jax.numpy as jnp
import numpy as np
from jax import lax

D = 1536
HEADS = 12
KV_HEADS = 2
HEAD_DIM = 128
FF = 768
EXPERTS = 32
TOP = 4
WINDOW = 2048
TOK_DEV = 256
REQ_DEV = 3
MOST = 128
SUB = 32
CAP = 8
TOKENS = 32768
REQUESTS = 384
N_DP = 16
N_EXPERT = 8
DEVICES = 128


def draw_key_cache(key, part):
    shape_all = (REQUESTS, WINDOW, KV_HEADS * HEAD_DIM)
    base = jnp.clip(jax.random.normal(key, shape_all, jnp.float32), -6.0, 6.0)
    return base.astype(jnp.bfloat16)


def with_ends(entries, own_key, smallest, top_value):
    dims = entries.shape
    index_at = [jax.random.randint(jax.random.fold_in(own_key, axis), (), 0, dims[axis]) for axis in range(len(dims))]
    entries = entries.at[tuple(index_at)].set(smallest)
    longest = dims.index(max(dims))
    index_at[longest] = (index_at[longest] + 1) % dims[longest]
    return entries.at[tuple(index_at)].set(top_value)


def block_levels(rng, extent, pieces, low, largest):
    gain = 1.0
    for axis_at, blocks in pieces:
        draws = jax.random.uniform(jax.random.fold_in(jax.random.fold_in(rng, 6), axis_at), (blocks,), jnp.float32, low / len(pieces), largest / len(pieces))
        gain = gain * jnp.repeat(jnp.exp(draws), extent[axis_at] // blocks).reshape((-1,) + (1,) * (len(extent) - 1 - axis_at))
    return gain


def length_profile(number_of, total, most, slope):
    portions = [(1 << 20) // math.isqrt(rank ** slope) + 1 for rank in range(2, number_of + 1)]
    rest, holding = total - most - (number_of - 1), [1] * (number_of - 1)
    while rest > 0:
        movable = [i for i in range(number_of - 1) if holding[i] < most]
        pool, budget = sum([portions[i] for i in movable]), rest
        for i in movable:
            addition = min(most - holding[i], max(1, budget * portions[i] // pool), rest)
            holding[i] = holding[i] + addition
            rest = rest - addition
    return np.array([most] + holding)


def uneven_parts(stream_key, number_of, total, reach, slope):
    if number_of == 2:
        one = jax.random.randint(stream_key, (), max(1, total - reach), min(reach, total - 1) + 1)
        return jnp.stack([one, total - one])
    tallies = jnp.asarray(length_profile(number_of, total, reach, slope), jnp.int32)
    pairs = (number_of - 1) // 2
    donor, sink = tallies[1:1 + 2 * pairs:2], tallies[2:2 + 2 * pairs:2]
    room = jnp.minimum(donor - 1, reach - sink)
    shifted = jax.random.randint(jax.random.fold_in(stream_key, 1), (pairs,), 0, 1 << 20) % (room + 1)
    tallies = tallies.at[1:1 + 2 * pairs:2].set(donor - shifted).at[2:2 + 2 * pairs:2].set(sink + shifted)
    return tallies[jax.random.permutation(jax.random.fold_in(stream_key, 2), number_of)]


def assign_block(stream_key, own, number, rows, amount, top, limit, slope):
    order = jax.random.permutation(stream_key, amount)
    crowded, common = shares(amount, rows * top, limit, slope, True), shares(amount, rows * top, limit, slope, False)
    places = jnp.arange(amount)

    def named(tallies, offset_by):
        used = int((tallies > 0).sum())
        fixed = max(1, used // 4)
        shifted = fixed + (places - fixed + offset_by * (used - fixed)) % max(1, amount - fixed)
        return jnp.zeros((amount,), jnp.int32).at[order[jnp.where(places < fixed, places, shifted)]].set(jnp.asarray(tallies, jnp.int32))

    tallies = jnp.where(number % 4 == 0, named(crowded, number // 4), named(common, number - number // 4 - 1))
    mixed = jax.random.permutation(jax.random.fold_in(own, 3), amount)
    donor, receiver = mixed[0:amount // 2 * 2:2], mixed[1:amount // 2 * 2:2]
    margin = jnp.minimum(tallies[donor] - 1, limit - tallies[receiver]) // 2
    margin = jnp.where((donor == order[0]) | (receiver == order[0]) | (tallies[receiver] == 0), 0, jnp.maximum(margin, 0))
    shifted = jax.random.randint(jax.random.fold_in(own, 4), (amount // 2,), 0, 1 << 20) % (margin + 1)
    tallies = tallies.at[donor].add(-shifted).at[receiver].add(shifted)
    members = jnp.searchsorted(jnp.cumsum(tallies), jnp.arange(rows * top), side="right").astype(jnp.int32)
    grid = members.reshape(top, rows).T
    grid = grid[jax.random.permutation(jax.random.fold_in(own, 1), rows)]
    offset_by = jax.random.randint(jax.random.fold_in(own, 2), (rows, 1), 0, top)
    return jnp.take_along_axis(grid, (jnp.arange(top)[None, :] + offset_by) % top, axis=1)


def shares(count, total, most, lean, full):
    weights = [(1 << 20) // math.isqrt(rank ** lean) + 1 for rank in range(1, count + 1)]
    largest = most if full else min(most, max(-(-total // count), total * weights[0] // sum(weights)))
    least = 1 if total - largest >= count - 1 else 0
    holding, rest = [largest] + [least] * (count - 1), total - largest - least * (count - 1)
    while rest > 0:
        candidates = [i for i in range(1, count) if holding[i] < largest] or [i for i in range(1, count) if holding[i] < most]
        pool, left = sum([weights[i] for i in candidates]), rest
        for i in candidates:
            more = min(most - holding[i], max(1, left * weights[i] // pool), rest)
            holding[i] = holding[i] + more
            rest = rest - more
    return np.array(holding)


def bell_draw(key, dims, width, reach, split=(), held_as=jnp.bfloat16):
    level = block_levels(key, dims, split, -0.22, 0.18) if split else 1.0
    drawn = jax.random.normal(key, dims, jnp.float32) * width * level
    return jnp.minimum(jnp.maximum(drawn, -reach), reach).astype(held_as)


def setup_inputs(seed: int = 0) -> dict:
    key_list = jax.random.split(jax.random.key(seed), 18)
    tokens = bell_draw(key_list[0], (TOKENS, D), 1.0, 6.0, ((0, 128),))
    attn_gain = jnp.clip(1.0 + 0.18 * jax.random.normal(key_list[1], (D,), jnp.float32), 0.1, 1.9)
    ffn_gain = jnp.clip(1.0 + 0.18 * jax.random.normal(key_list[2], (D,), jnp.float32), 0.1, 1.9)
    w_query = bell_draw(key_list[3], (D, HEADS * HEAD_DIM), D ** -0.5, 0.15625)
    w_key = bell_draw(key_list[4], (D, KV_HEADS * HEAD_DIM), D ** -0.5, 0.15625)
    w_value = bell_draw(key_list[5], (D, KV_HEADS * HEAD_DIM), D ** -0.5, 0.15625)
    w_out = bell_draw(key_list[6], (HEADS * HEAD_DIM, D), (HEADS * HEAD_DIM) ** -0.5, 0.15625)
    key_cache = draw_key_cache(jax.random.fold_in(key_list[17], 71), 0)
    value_cache = bell_draw(key_list[8], (REQUESTS, WINDOW, KV_HEADS * HEAD_DIM), 1.0, 6.0, ((0, 128),))
    req_lengths = jax.vmap(lambda own: uneven_parts(own, REQ_DEV, TOK_DEV, MOST, 2))(jax.random.split(key_list[9], DEVICES)).reshape((DEVICES, REQ_DEV)).astype(jnp.int32)
    cache_lengths = with_ends(jax.random.randint(key_list[10], (DEVICES, REQ_DEV), WINDOW // 2, WINDOW + 1), jax.random.fold_in(key_list[10], 1), WINDOW // 2, WINDOW).astype(jnp.int32)
    expert_ids_keys = jax.random.split(jax.random.fold_in(key_list[11], 1), TOKENS // SUB)
    expert_ids_turns = jax.random.permutation(jax.random.fold_in(key_list[11], 3), TOKENS // SUB)
    expert_ids = jax.vmap(lambda own, number: assign_block(jax.random.fold_in(key_list[11], 2), own, number, SUB, EXPERTS, TOP, CAP, 2))(expert_ids_keys, expert_ids_turns).reshape((TOKENS, TOP))
    route_gate = jnp.clip(0.1 + 0.9 * jax.random.uniform(key_list[12], (TOKENS, TOP), jnp.float32) ** block_levels(key_list[12], (TOKENS, TOP), ((0, 128),), -0.2, 0.2), 0.1, 1.0)
    replica_owner = jax.vmap(lambda own: jax.random.permutation(own, N_EXPERT))(jax.random.split(key_list[13], EXPERTS)).reshape((EXPERTS, N_EXPERT)).astype(jnp.int32)
    replica_pick = jax.vmap(lambda own: jax.random.permutation(own, N_EXPERT))(jax.random.split(key_list[14], DEVICES)).reshape((DEVICES, N_EXPERT)).astype(jnp.int32)
    w_gate_up = bell_draw(key_list[15], (EXPERTS, FF, 2, D), D ** -0.5, 0.15625, ((0, 16), (1, 8)))
    w_down = bell_draw(key_list[16], (EXPERTS, D, FF), FF ** -0.5, 0.21875, ((0, 16), (1, 8)))
    return {"tokens": tokens, "attn_gain": attn_gain, "ffn_gain": ffn_gain, "w_query": w_query, "w_key": w_key, "w_value": w_value, "w_out": w_out, "key_cache": key_cache, "value_cache": value_cache, "req_lengths": req_lengths, "cache_lengths": cache_lengths, "expert_ids": expert_ids, "route_gate": route_gate, "replica_owner": replica_owner, "replica_pick": replica_pick, "w_gate_up": w_gate_up, "w_down": w_down}


epsilon = 1e-06
rope_base = 1000000.0

def rms_scale(values_in, gain_vec):
    widened = values_in.astype(jnp.float32)
    mean_square = lax.optimization_barrier(jnp.mean(widened * widened, axis=-1, keepdims=True))
    return (widened * lax.rsqrt(mean_square + epsilon) * gain_vec).astype(jnp.bfloat16)

def rotate(projected, positions, head_count):
    half_dim = HEAD_DIM // 2
    shaped = projected.reshape(projected.shape[0], head_count, HEAD_DIM)
    inverse = rope_base ** (-(jnp.arange(half_dim, dtype=jnp.float32) * 2.0 / HEAD_DIM))
    angles = positions.astype(jnp.float32)[:, None] * inverse[None, :]
    cosine = jnp.cos(angles)[:, None, :]
    sine_part = jnp.sin(angles)[:, None, :]
    first_half = shaped[..., :half_dim]
    second_half = shaped[..., half_dim:]
    turned = jnp.concatenate([first_half * cosine - second_half * sine_part, second_half * cosine + first_half * sine_part], axis=-1)
    return turned.reshape(projected.shape).astype(jnp.bfloat16)

def attend_device(tokens_dev, lengths_dev, cache_dev, key_cache_dev, value_cache_dev, attn_gain, w_query, w_key, w_value, w_out):
    token_count = tokens_dev.shape[0]
    longest = token_count // 2
    request_count = lengths_dev.shape[0]
    group_size = HEADS // KV_HEADS
    normed_in = rms_scale(tokens_dev, attn_gain)
    starts = jnp.cumsum(lengths_dev).astype(jnp.int32) - lengths_dev
    token_index = jnp.arange(token_count, dtype=jnp.int32)
    request_of = lax.optimization_barrier(jnp.sum((token_index[:, None] >= starts[None, 1:]).astype(jnp.int32), axis=1))
    pick_request = (request_of[:, None] == jnp.arange(request_count, dtype=jnp.int32)[None, :]).astype(jnp.int32)
    offset_in = token_index - lax.optimization_barrier(jnp.sum(pick_request * starts[None, :], axis=1))
    positions = lax.optimization_barrier(jnp.sum(pick_request * cache_dev[None, :], axis=1)) + offset_in
    queries = rotate(jnp.dot(normed_in, w_query, preferred_element_type=jnp.float32), positions, HEADS)
    key_new = rotate(jnp.dot(normed_in, w_key, preferred_element_type=jnp.float32), positions, KV_HEADS)
    value_new = jnp.dot(normed_in, w_value, preferred_element_type=jnp.float32).astype(jnp.bfloat16)
    queries_pad = jnp.concatenate([queries, jnp.zeros((longest, queries.shape[1]), jnp.bfloat16)], axis=0)
    keys_pad = jnp.concatenate([key_new, jnp.zeros((longest, key_new.shape[1]), jnp.bfloat16)], axis=0)
    values_pad = jnp.concatenate([value_new, jnp.zeros((longest, value_new.shape[1]), jnp.bfloat16)], axis=0)
    window_size = key_cache_dev.shape[1]
    outputs_list = []
    for request in range(request_count):
        first_row = starts[request]
        length_here = lengths_dev[request]
        cached_here = cache_dev[request]
        query_block = lax.dynamic_slice_in_dim(queries_pad, first_row, longest, 0)
        key_block = jnp.concatenate([key_cache_dev[request], lax.dynamic_slice_in_dim(keys_pad, first_row, longest, 0)], axis=0)
        value_block = jnp.concatenate([value_cache_dev[request], lax.dynamic_slice_in_dim(values_pad, first_row, longest, 0)], axis=0)
        slot_index = jnp.arange(window_size, dtype=jnp.int32)
        new_index = jnp.arange(longest, dtype=jnp.int32)
        key_position = jnp.concatenate([slot_index, cached_here + new_index])
        key_valid = jnp.concatenate([slot_index < cached_here, new_index < length_here])
        query_position = cached_here + new_index
        allowed = key_valid[None, :] & (key_position[None, :] <= query_position[:, None]) & ((key_position[None, :] == 0) | (query_position[:, None] - key_position[None, :] < window_size))
        query_heads = query_block.reshape(longest, KV_HEADS, group_size, HEAD_DIM).astype(jnp.float32)
        key_heads = key_block.reshape(-1, KV_HEADS, HEAD_DIM).astype(jnp.float32)
        value_heads = value_block.reshape(-1, KV_HEADS, HEAD_DIM).astype(jnp.float32)
        scores = jnp.einsum('qgsd,kgd->gsqk', query_heads, key_heads) * HEAD_DIM ** (-0.5)
        scores = jnp.where(allowed[None, None], scores, -jnp.inf)
        row_peak = lax.optimization_barrier(jnp.max(scores, axis=-1, keepdims=True))
        exponent = jnp.exp(scores - row_peak)
        weights = (exponent / lax.optimization_barrier(jnp.sum(exponent, axis=-1, keepdims=True))).astype(jnp.bfloat16)
        attended = jnp.einsum('gsqk,kgd->qgsd', weights.astype(jnp.float32), value_heads)
        outputs_list.append(attended.reshape(longest, HEADS * HEAD_DIM).astype(jnp.bfloat16))
    stacked = jnp.concatenate(outputs_list, axis=0)
    gathered = stacked[request_of * longest + offset_in]
    projected = jnp.dot(gathered, w_out, preferred_element_type=jnp.float32)
    return (tokens_dev.astype(jnp.float32) + projected).astype(jnp.bfloat16)

def reference(tokens, attn_gain, ffn_gain, w_query, w_key, w_value, w_out, key_cache, value_cache, req_lengths, cache_lengths, expert_ids, route_gate, replica_owner, replica_pick, w_gate_up, w_down):
    device_count = N_DP * N_EXPERT
    per_device = tokens.shape[0] // device_count
    request_count = req_lengths.shape[1]
    tokens_split = tokens.reshape(device_count, per_device, tokens.shape[1])
    keys_split = key_cache.reshape(device_count, request_count, key_cache.shape[1], key_cache.shape[2])
    values_split = value_cache.reshape(device_count, request_count, value_cache.shape[1], value_cache.shape[2])

    def one_device(packed):
        return attend_device(packed[0], packed[1], packed[2], packed[3], packed[4], attn_gain, w_query, w_key, w_value, w_out)
    residual = lax.map(one_device, (tokens_split, req_lengths, cache_lengths, keys_split, values_split)).reshape(tokens.shape)
    normed_mid = rms_scale(residual, ffn_gain)
    top_count = expert_ids.shape[1]
    route_count = expert_ids.shape[0] * top_count
    expert_flat = expert_ids.reshape(-1)
    gate_flat = route_gate.reshape(-1)
    route_token = jnp.arange(route_count, dtype=jnp.int32) // top_count
    per_expert = jax.ops.segment_sum(jnp.ones_like(expert_flat), expert_flat, num_segments=EXPERTS)
    expert_start = (jnp.cumsum(per_expert) - per_expert).astype(jnp.int32)
    route_order = jnp.argsort(expert_flat, stable=True).astype(jnp.int32)
    capacity = tokens.shape[0] // SUB * CAP
    order_pad = jnp.concatenate([route_order, jnp.zeros((capacity,), jnp.int32)])

    def add_expert(running_sum, expert):
        chosen = lax.dynamic_slice_in_dim(order_pad, expert_start[expert], capacity, 0)
        is_used = jnp.arange(capacity, dtype=jnp.int32) < per_expert[expert]
        chosen_tokens = route_token[chosen]
        token_rows = normed_mid[chosen_tokens]
        gate_up = w_gate_up[expert]
        gate_part = jnp.dot(token_rows, gate_up[:, 0, :].T, preferred_element_type=jnp.float32)
        up_part = jnp.dot(token_rows, gate_up[:, 1, :].T, preferred_element_type=jnp.float32)
        hidden = (jnp.maximum(gate_part, 0.0) * up_part).astype(jnp.bfloat16)
        expert_out = jnp.dot(hidden, w_down[expert].T, preferred_element_type=jnp.float32).astype(jnp.bfloat16)
        scaled = jnp.where(is_used, gate_flat[chosen], 0.0)[:, None] * expert_out.astype(jnp.float32)
        return (running_sum.at[chosen_tokens].add(scaled), None)
    mixed_sum, ignored = lax.scan(add_expert, jnp.zeros(tokens.shape, jnp.float32), jnp.arange(EXPERTS, dtype=jnp.int32))
    layer_out = (residual.astype(jnp.float32) + mixed_sum).astype(jnp.bfloat16)
    local_experts = EXPERTS // N_DP
    block_of = route_token % per_device // SUB
    source = route_token // per_device
    replica = replica_pick[source, block_of]
    owner_axis = replica_owner[expert_flat, replica]
    owner_device = expert_flat // local_experts * N_EXPERT + owner_axis
    slot_key = owner_device * local_experts + expert_flat % local_experts
    owner_rows = jax.ops.segment_sum(jnp.ones_like(slot_key), slot_key, num_segments=device_count * local_experts).reshape(device_count, local_experts)
    return (layer_out, owner_rows)
```

```python
import functools

import jax
import jax.numpy as jnp
from jax import lax
from jax.experimental import pallas as pl
from jax.experimental.pallas import tpu as pltpu
from jax.sharding import PartitionSpec as P

HEADS = 12
KV_HEADS = 2
HEAD_DIM = 128


epsilon = 1e-06
rope_base = 1000000.0


def rms_scale(values_in, gain_vec):
    widened = values_in.astype(jnp.float32)
    mean_square = jnp.mean(widened * widened, axis=-1, keepdims=True)
    return (widened * lax.rsqrt(mean_square + epsilon) * gain_vec).astype(jnp.bfloat16)


def rotate(projected, positions, head_count):
    half_dim = HEAD_DIM // 2
    shaped = projected.reshape(projected.shape[0], head_count, HEAD_DIM)
    inverse = rope_base ** (-(jnp.arange(half_dim, dtype=jnp.float32) * 2.0 / HEAD_DIM))
    angles = positions.astype(jnp.float32)[:, None] * inverse[None, :]
    cosine = jnp.cos(angles)[:, None, :]
    sine_part = jnp.sin(angles)[:, None, :]
    first_half = shaped[..., :half_dim]
    second_half = shaped[..., half_dim:]
    turned = jnp.concatenate(
        [
            first_half * cosine - second_half * sine_part,
            second_half * cosine + first_half * sine_part,
        ],
        axis=-1,
    )
    return turned.reshape(projected.shape).astype(jnp.bfloat16)


def attend_device(
    tokens_dev,
    lengths_dev,
    cache_dev,
    key_cache_dev,
    value_cache_dev,
    attn_gain,
    w_query,
    w_key,
    w_value,
    w_out,
):
    token_count = tokens_dev.shape[0]
    longest = token_count // 2
    request_count = lengths_dev.shape[0]
    group_size = HEADS // KV_HEADS
    normed_in = rms_scale(tokens_dev, attn_gain)
    starts = jnp.cumsum(lengths_dev) - lengths_dev
    token_index = jnp.arange(token_count, dtype=jnp.int32)
    request_of = jnp.sum((token_index[:, None] >= starts[None, 1:]).astype(jnp.int32), axis=1)
    pick_request = (
        request_of[:, None] == jnp.arange(request_count, dtype=jnp.int32)[None, :]
    ).astype(jnp.int32)
    offset_in = token_index - jnp.sum(pick_request * starts[None, :], axis=1)
    positions = jnp.sum(pick_request * cache_dev[None, :], axis=1) + offset_in
    queries = rotate(
        jnp.dot(normed_in, w_query, preferred_element_type=jnp.float32), positions, HEADS
    )
    key_new = rotate(
        jnp.dot(normed_in, w_key, preferred_element_type=jnp.float32), positions, KV_HEADS
    )
    value_new = jnp.dot(normed_in, w_value, preferred_element_type=jnp.float32).astype(jnp.bfloat16)
    queries_pad = jnp.concatenate(
        [queries, jnp.zeros((longest, queries.shape[1]), jnp.bfloat16)], axis=0
    )
    keys_pad = jnp.concatenate(
        [key_new, jnp.zeros((longest, key_new.shape[1]), jnp.bfloat16)], axis=0
    )
    values_pad = jnp.concatenate(
        [value_new, jnp.zeros((longest, value_new.shape[1]), jnp.bfloat16)], axis=0
    )
    window_size = key_cache_dev.shape[1]
    outputs_list = []
    for request in range(request_count):
        first_row = starts[request]
        length_here = lengths_dev[request]
        cached_here = cache_dev[request]
        query_block = lax.dynamic_slice_in_dim(queries_pad, first_row, longest, 0)
        key_block = jnp.concatenate(
            [key_cache_dev[request], lax.dynamic_slice_in_dim(keys_pad, first_row, longest, 0)],
            axis=0,
        )
        value_block = jnp.concatenate(
            [value_cache_dev[request], lax.dynamic_slice_in_dim(values_pad, first_row, longest, 0)],
            axis=0,
        )
        slot_index = jnp.arange(window_size, dtype=jnp.int32)
        new_index = jnp.arange(longest, dtype=jnp.int32)
        key_position = jnp.concatenate([slot_index, cached_here + new_index])
        key_valid = jnp.concatenate([slot_index < cached_here, new_index < length_here])
        query_position = cached_here + new_index
        allowed = (
            key_valid[None, :]
            & (key_position[None, :] <= query_position[:, None])
            & (
                (key_position[None, :] == 0)
                | (query_position[:, None] - key_position[None, :] < window_size)
            )
        )
        query_heads = query_block.reshape(longest, KV_HEADS, group_size, HEAD_DIM)
        key_heads = key_block.reshape(-1, KV_HEADS, HEAD_DIM)
        value_heads = value_block.reshape(-1, KV_HEADS, HEAD_DIM)
        scores = jnp.einsum(
            "qgsd,kgd->gsqk", query_heads, key_heads, preferred_element_type=jnp.float32
        ) * HEAD_DIM ** (-0.5)
        scores = jnp.where(allowed[None, None], scores, -jnp.inf)
        row_peak = jnp.max(scores, axis=-1, keepdims=True)
        exponent = jnp.exp(scores - row_peak)
        weights = (exponent / jnp.sum(exponent, axis=-1, keepdims=True)).astype(jnp.bfloat16)
        attended = jnp.einsum(
            "gsqk,kgd->qgsd", weights, value_heads, preferred_element_type=jnp.float32
        )
        outputs_list.append(attended.reshape(longest, HEADS * HEAD_DIM).astype(jnp.bfloat16))
    stacked = jnp.concatenate(outputs_list, axis=0)
    gathered = stacked[request_of * longest + offset_in]
    projected = jnp.dot(gathered, w_out, preferred_element_type=jnp.float32)
    return (tokens_dev.astype(jnp.float32) + projected).astype(jnp.bfloat16)


MESH = pl.DeviceIdType.MESH
SIDE = 4
SLOTS = 32
HALF = 128
WIDTH = 1536
PARTNERS = [
    (dz, dx, dc)
    for dz in range(SIDE)
    for dx in range(SIDE)
    for dc in range(2)
    if (dz == 0 or dx == 0) and (dz, dx, dc) != (0, 0, 0)
]


def place():
    row, column = lax.axis_index("dp"), lax.axis_index("expert")
    return row // SIDE, row % SIDE, column // 2, column % 2


def device_at(dz, dx, dc):
    z, x, y, c = place()
    row = ((z + dz) % SIDE) * SIDE + (x + dx) % SIDE
    return (row, y * 2 + (c + dc) % 2)


def along(half, offset, dc=0):
    return device_at(0, offset, dc) if half == 0 else device_at(offset, 0, dc)


def across(half, offset):
    return device_at(offset, 0, 0) if half == 0 else device_at(0, offset, 0)


def source_row(half, back):
    z, x, _, _ = place()
    if half == 0:
        return ((z + SIDE - back) % SIDE) * SIDE + x
    return z * SIDE + (x + SIDE - back) % SIDE


def greet():
    barrier = pltpu.get_barrier_semaphore()
    for offsets in PARTNERS:
        pl.semaphore_signal(barrier, inc=1, device_id=device_at(*offsets), device_id_type=MESH)
    pl.semaphore_wait(barrier, len(PARTNERS))


def dispatch_kernel(rows_ref, table_ref, out_ref, held, packed, sem_s1, sem_r1, sem_s2, sem_r2, sem_own):
    z, x, y, c = place()
    greet()
    first = {}
    for back in (1, 3, 2):
        for half in range(2):
            first[half, back] = pltpu.make_async_remote_copy(
                src_ref=rows_ref.at[pl.ds(half * HALF, HALF)],
                dst_ref=held.at[half, back],
                send_sem=sem_s1.at[half, back],
                recv_sem=sem_r1.at[half, back],
                device_id=across(half, back),
                device_id_type=MESH,
            )
            first[half, back].start()
    second = []
    line = lax.broadcasted_iota(jnp.int32, (8 * SLOTS, HALF), 0)
    for back in (0, 1, 3, 2):
        for half in range(2):
            if back:
                first[half, back].wait_recv()
                chunk = held[half, back]
            else:
                chunk = rows_ref[pl.ds(half * HALF, HALF), :]
            if half == 0:
                wanted = line + z * 256
            else:
                wanted = (line // 64) * 256 + x * 64 + line % 64
            table = table_ref[source_row(half, back)]
            hot = jnp.zeros((8 * SLOTS, HALF), jnp.bool_)
            for k in range(4):
                code = table[k : k + 1, half * HALF : (half + 1) * HALF].astype(jnp.int32)
                hot = hot | (code == wanted)
            spread = jnp.dot(
                hot.astype(jnp.float32).astype(jnp.bfloat16), chunk, preferred_element_type=jnp.float32
            ).astype(jnp.bfloat16)
            packed[half, back] = spread.reshape(SIDE, 2, SLOTS, WIDTH)
            for dc in (1, 0):
                for offset in (2, 1, 3, 0):
                    at = (x if half == 0 else z) + offset
                    piece = packed.at[half, back, at % SIDE, (c + dc) % 2]
                    landing = out_ref.at[half, offset, dc, back]
                    if offset == 0 and dc == 0:
                        copy = pltpu.make_async_copy(piece, landing, sem_own.at[half, back])
                    else:
                        copy = pltpu.make_async_remote_copy(
                            src_ref=piece,
                            dst_ref=landing,
                            send_sem=sem_s2.at[half, back, offset, dc],
                            recv_sem=sem_r2.at[half, back, offset, dc],
                            device_id=along(half, offset, dc),
                            device_id_type=MESH,
                        )
                    copy.start()
                    second.append(copy)
    for copy in first.values():
        copy.wait_send()
    for copy in second:
        copy.wait()


def dispatch(rows, table):
    any_space = pl.BlockSpec(memory_space=pl.ANY)
    vmem = pl.BlockSpec(memory_space=pltpu.VMEM)
    return pl.pallas_call(
        dispatch_kernel,
        out_shape=jax.ShapeDtypeStruct((2, SIDE, 2, SIDE, SLOTS, WIDTH), jnp.bfloat16),
        in_specs=[vmem, vmem],
        out_specs=any_space,
        scratch_shapes=[
            pltpu.VMEM((2, SIDE, HALF, WIDTH), jnp.bfloat16),
            pltpu.VMEM((2, SIDE, SIDE, 2, SLOTS, WIDTH), jnp.bfloat16),
            pltpu.SemaphoreType.DMA((2, SIDE)),
            pltpu.SemaphoreType.DMA((2, SIDE)),
            pltpu.SemaphoreType.DMA((2, SIDE, SIDE, 2)),
            pltpu.SemaphoreType.DMA((2, SIDE, SIDE, 2)),
            pltpu.SemaphoreType.DMA((2, SIDE)),
        ],
        name="dispatch",
        compiler_params=pltpu.CompilerParams(
            collective_id=1, has_side_effects=True, vmem_limit_bytes=40 << 20
        ),
    )(rows, table)


def combine_kernel(done_ref, table_ref, residual_ref, out_ref, back_rows, partial, given, total, sem_s1, sem_r1, sem_own, sem_s2, sem_r2):
    z, x, y, c = place()
    greet()
    first = {}
    for back in (2, 1, 3, 0):
        for half in range(2):
            for dc in (1, 0):
                for offset in (2, 1, 3, 0):
                    piece = done_ref.at[half, offset, dc, back]
                    landing = back_rows.at[half, back, offset, dc]
                    if offset == 0 and dc == 0:
                        copy = pltpu.make_async_copy(piece, landing, sem_own.at[half, back])
                    else:
                        copy = pltpu.make_async_remote_copy(
                            src_ref=piece,
                            dst_ref=landing,
                            send_sem=sem_s1.at[half, back, offset, dc],
                            recv_sem=sem_r1.at[half, back, offset, dc],
                            device_id=along(half, SIDE - offset, dc),
                            device_id_type=MESH,
                        )
                    copy.start()
                    first[half, back, offset, dc] = copy
    line = lax.broadcasted_iota(jnp.int32, (8 * SLOTS, HALF), 0)
    turn, swap, slot = line // 64, (line // 32) % 2, line % 32
    second = {}
    for back in (2, 1, 3, 0):
        for half in range(2):
            for offset in range(SIDE):
                for dc in range(2):
                    copy = first[half, back, offset, dc]
                    if offset == 0 and dc == 0:
                        copy.wait()
                    else:
                        copy.wait_recv()
            if half == 0:
                owner = z * SIDE + (x + turn) % SIDE
            else:
                owner = ((z + turn) % SIDE) * SIDE + x
            wanted = owner * 64 + ((c + swap) % 2) * 32 + slot
            table = table_ref[source_row(half, back)]
            weight = jnp.zeros((8 * SLOTS, HALF), jnp.float32)
            for k in range(4):
                code = table[k : k + 1, half * HALF : (half + 1) * HALF].astype(jnp.int32)
                gate = table[4 + k : 5 + k, half * HALF : (half + 1) * HALF]
                weight = weight + jnp.where(code == wanted, gate, 0.0)
            coarse = weight.astype(jnp.bfloat16)
            fine = (weight - coarse.astype(jnp.float32)).astype(jnp.bfloat16)
            landed = back_rows[half, back].reshape(8 * SLOTS, WIDTH)
            dims = (((0,), (0,)), ((), ()))
            mixed = lax.dot_general(
                coarse, landed, dims, preferred_element_type=jnp.float32
            ) + lax.dot_general(fine, landed, dims, preferred_element_type=jnp.float32)
            if back == 0:
                total[half] = mixed
            else:
                partial[half, back] = mixed.astype(jnp.bfloat16)
                second[half, back] = pltpu.make_async_remote_copy(
                    src_ref=partial.at[half, back],
                    dst_ref=given.at[half, back],
                    send_sem=sem_s2.at[half, back],
                    recv_sem=sem_r2.at[half, back],
                    device_id=across(half, SIDE - back),
                    device_id_type=MESH,
                )
                second[half, back].start()
    for half in range(2):
        mixed = total[half]
        for back in (2, 1, 3):
            second[half, back].wait_recv()
            mixed = mixed + given[half, back].astype(jnp.float32)
        here = pl.ds(half * HALF, HALF)
        out_ref[here, :] = (residual_ref[here, :].astype(jnp.float32) + mixed).astype(jnp.bfloat16)
    for key, copy in first.items():
        if key[2:] != (0, 0):
            copy.wait_send()
    for copy in second.values():
        copy.wait_send()


def combine(done, table, residual):
    any_space = pl.BlockSpec(memory_space=pl.ANY)
    vmem = pl.BlockSpec(memory_space=pltpu.VMEM)
    return pl.pallas_call(
        combine_kernel,
        out_shape=jax.ShapeDtypeStruct((2 * HALF, WIDTH), jnp.bfloat16),
        in_specs=[any_space, vmem, vmem],
        out_specs=vmem,
        scratch_shapes=[
            pltpu.VMEM((2, SIDE, SIDE, 2, SLOTS, WIDTH), jnp.bfloat16),
            pltpu.VMEM((2, SIDE, HALF, WIDTH), jnp.bfloat16),
            pltpu.VMEM((2, SIDE, HALF, WIDTH), jnp.bfloat16),
            pltpu.VMEM((2, HALF, WIDTH), jnp.float32),
            pltpu.SemaphoreType.DMA((2, SIDE, SIDE, 2)),
            pltpu.SemaphoreType.DMA((2, SIDE, SIDE, 2)),
            pltpu.SemaphoreType.DMA((2, SIDE)),
            pltpu.SemaphoreType.DMA((2, SIDE)),
            pltpu.SemaphoreType.DMA((2, SIDE)),
        ],
        name="combine",
        compiler_params=pltpu.CompilerParams(
            collective_id=2, has_side_effects=True, vmem_limit_bytes=48 << 20
        ),
    )(done, table, residual)


def gather_own_expert(shards):
    core = lax.axis_index("expert") % 2
    axis_count = lax.axis_size("expert")
    mine = lax.dynamic_index_in_dim(shards, core, 0, keepdims=False)
    other = lax.dynamic_index_in_dim(shards, 1 - core, 0, keepdims=False)
    swapped = lax.ppermute(other, "expert", [(i, i ^ 1) for i in range(axis_count)])
    pair = jnp.stack([jnp.where(core == 0, mine, swapped), jnp.where(core == 0, swapped, mine)])
    groups = [list(range(k, axis_count, 2)) for k in range(2)]
    return lax.all_gather(pair, "expert", axis=0, axis_index_groups=groups, tiled=True)


def on_device(
    tokens,
    attn_gain,
    ffn_gain,
    w_query,
    w_key,
    w_value,
    w_out,
    key_cache,
    value_cache,
    req_lengths,
    cache_lengths,
    expert_ids,
    route_gate,
    replica_owner,
    replica_pick,
    w_gate_up,
    w_down,
):
    dp_count = lax.axis_size("dp")
    axis_count = lax.axis_size("expert")
    device_count = dp_count * axis_count
    local_experts = w_gate_up.shape[0]
    token_count = tokens.shape[0]
    expert_total = replica_owner.shape[0]
    sub_rows = token_count // axis_count

    experts = jnp.arange(expert_total, dtype=jnp.int32)
    route_hot = (expert_ids[:, :, None] == experts).astype(jnp.int32)
    blocked = jnp.sum(route_hot, axis=1).reshape(axis_count, sub_rows, expert_total)
    earlier = (
        jnp.arange(sub_rows, dtype=jnp.int32)[:, None] > jnp.arange(sub_rows, dtype=jnp.int32)[None, :]
    ).astype(jnp.bfloat16)
    before = jnp.einsum(
        "ts,bsx->btx", earlier, blocked.astype(jnp.bfloat16), preferred_element_type=jnp.float32
    ).reshape(token_count, 1, expert_total)
    rank = jnp.sum(route_hot.astype(jnp.float32) * before, axis=2)
    block_in_half = (jnp.arange(token_count, dtype=jnp.int32) // sub_rows) % 4
    codes = (expert_ids * SLOTS + block_in_half[:, None] * 8).astype(jnp.float32) + rank
    mine = jnp.concatenate([codes.T, route_gate.T], axis=0)
    table = lax.all_gather(mine, "dp", axis=0, tiled=False)

    per_block = jnp.sum(blocked, axis=1)
    picked = (
        replica_pick[0][:, None] == jnp.arange(axis_count, dtype=jnp.int32)[None, :]
    ).astype(jnp.int32)
    owned = (
        replica_owner[:, :, None] == jnp.arange(axis_count, dtype=jnp.int32)[None, None, :]
    ).astype(jnp.int32)
    by_replica = jnp.sum(picked[:, None, :] * per_block[:, :, None], axis=0)
    by_owner = jnp.sum(by_replica[:, :, None] * owned, axis=1)
    send_counts = (
        by_owner.reshape(dp_count, local_experts, axis_count)
        .transpose(0, 2, 1)
        .reshape(device_count, local_experts)
    )
    owner_rows = lax.psum_scatter(send_counts, ("dp", "expert"), scatter_dimension=0, tiled=True)

    gate_up = gather_own_expert(w_gate_up).reshape(-1, 2, WIDTH)
    down_shards = gather_own_expert(w_down)
    down = down_shards.reshape(WIDTH, -1)

    residual = attend_device(
        tokens,
        req_lengths[0],
        cache_lengths[0],
        key_cache,
        value_cache,
        attn_gain,
        w_query,
        w_key,
        w_value,
        w_out,
    )
    normed_mid = rms_scale(residual, ffn_gain)
    arrived = dispatch(normed_mid, table)
    both_parts = jnp.einsum(
        "rd,fcd->crf", arrived.reshape(-1, WIDTH), gate_up, preferred_element_type=jnp.float32
    )
    hidden = (jnp.maximum(both_parts[0], 0.0) * both_parts[1]).astype(jnp.bfloat16)
    expert_out = jnp.einsum(
        "rf,nf->rn", hidden, down, preferred_element_type=jnp.float32
    ).astype(jnp.bfloat16)
    layer_out = combine(expert_out.reshape(arrived.shape), table, residual)
    return (layer_out, owner_rows)


def solution(mesh):
    in_specs = (
        P(("dp", "expert"), None),
        P(),
        P(),
        P(),
        P(),
        P(),
        P(),
        P(("dp", "expert"), None, None),
        P(("dp", "expert"), None, None),
        P(("dp", "expert"), None),
        P(("dp", "expert"), None),
        P(("dp", "expert"), None),
        P(("dp", "expert"), None),
        P(),
        P(("dp", "expert"), None),
        P("dp", "expert", None, None),
        P("dp", "expert", None),
    )
    out_specs = (P(("dp", "expert"), None), P(("dp", "expert"), None))
    return jax.shard_map(
        on_device, mesh=mesh, in_specs=in_specs, out_specs=out_specs, check_vma=False
    )
```

```python
import functools

import jax
import jax.numpy as jnp
from jax import lax
from jax.experimental import pallas as pl
from jax.experimental.pallas import tpu as pltpu
from jax.sharding import PartitionSpec as P

HEADS = 12
KV_HEADS = 2
HEAD_DIM = 128


epsilon = 1e-06
rope_base = 1000000.0


def rms_scale(values_in, gain_vec):
    widened = values_in.astype(jnp.float32)
    mean_square = jnp.mean(widened * widened, axis=-1, keepdims=True)
    return (widened * lax.rsqrt(mean_square + epsilon) * gain_vec).astype(jnp.bfloat16)


def rotate(projected, positions, head_count):
    half_dim = HEAD_DIM // 2
    shaped = projected.reshape(projected.shape[0], head_count, HEAD_DIM)
    inverse = rope_base ** (-(jnp.arange(half_dim, dtype=jnp.float32) * 2.0 / HEAD_DIM))
    angles = positions.astype(jnp.float32)[:, None] * inverse[None, :]
    cosine = jnp.cos(angles)[:, None, :]
    sine_part = jnp.sin(angles)[:, None, :]
    first_half = shaped[..., :half_dim]
    second_half = shaped[..., half_dim:]
    turned = jnp.concatenate(
        [
            first_half * cosine - second_half * sine_part,
            second_half * cosine + first_half * sine_part,
        ],
        axis=-1,
    )
    return turned.reshape(projected.shape).astype(jnp.bfloat16)


def attend_device(
    tokens_dev,
    lengths_dev,
    cache_dev,
    key_cache_dev,
    value_cache_dev,
    attn_gain,
    w_query,
    w_key,
    w_value,
    w_out,
):
    token_count = tokens_dev.shape[0]
    longest = token_count // 2
    request_count = lengths_dev.shape[0]
    group_size = HEADS // KV_HEADS
    normed_in = rms_scale(tokens_dev, attn_gain)
    starts = jnp.cumsum(lengths_dev) - lengths_dev
    token_index = jnp.arange(token_count, dtype=jnp.int32)
    request_of = jnp.sum((token_index[:, None] >= starts[None, 1:]).astype(jnp.int32), axis=1)
    pick_request = (
        request_of[:, None] == jnp.arange(request_count, dtype=jnp.int32)[None, :]
    ).astype(jnp.int32)
    offset_in = token_index - jnp.sum(pick_request * starts[None, :], axis=1)
    positions = jnp.sum(pick_request * cache_dev[None, :], axis=1) + offset_in
    queries = rotate(
        jnp.dot(normed_in, w_query, preferred_element_type=jnp.float32), positions, HEADS
    )
    key_new = rotate(
        jnp.dot(normed_in, w_key, preferred_element_type=jnp.float32), positions, KV_HEADS
    )
    value_new = jnp.dot(normed_in, w_value, preferred_element_type=jnp.float32).astype(jnp.bfloat16)
    queries_pad = jnp.concatenate(
        [queries, jnp.zeros((longest, queries.shape[1]), jnp.bfloat16)], axis=0
    )
    keys_pad = jnp.concatenate(
        [key_new, jnp.zeros((longest, key_new.shape[1]), jnp.bfloat16)], axis=0
    )
    values_pad = jnp.concatenate(
        [value_new, jnp.zeros((longest, value_new.shape[1]), jnp.bfloat16)], axis=0
    )
    window_size = key_cache_dev.shape[1]
    outputs_list = []
    for request in range(request_count):
        first_row = starts[request]
        length_here = lengths_dev[request]
        cached_here = cache_dev[request]
        query_block = lax.dynamic_slice_in_dim(queries_pad, first_row, longest, 0)
        key_block = jnp.concatenate(
            [key_cache_dev[request], lax.dynamic_slice_in_dim(keys_pad, first_row, longest, 0)],
            axis=0,
        )
        value_block = jnp.concatenate(
            [value_cache_dev[request], lax.dynamic_slice_in_dim(values_pad, first_row, longest, 0)],
            axis=0,
        )
        slot_index = jnp.arange(window_size, dtype=jnp.int32)
        new_index = jnp.arange(longest, dtype=jnp.int32)
        key_position = jnp.concatenate([slot_index, cached_here + new_index])
        key_valid = jnp.concatenate([slot_index < cached_here, new_index < length_here])
        query_position = cached_here + new_index
        allowed = (
            key_valid[None, :]
            & (key_position[None, :] <= query_position[:, None])
            & (
                (key_position[None, :] == 0)
                | (query_position[:, None] - key_position[None, :] < window_size)
            )
        )
        query_heads = query_block.reshape(longest, KV_HEADS, group_size, HEAD_DIM)
        key_heads = key_block.reshape(-1, KV_HEADS, HEAD_DIM)
        value_heads = value_block.reshape(-1, KV_HEADS, HEAD_DIM)
        scores = jnp.einsum(
            "qgsd,kgd->gsqk", query_heads, key_heads, preferred_element_type=jnp.float32
        ) * HEAD_DIM ** (-0.5)
        scores = jnp.where(allowed[None, None], scores, -jnp.inf)
        row_peak = jnp.max(scores, axis=-1, keepdims=True)
        exponent = jnp.exp(scores - row_peak)
        weights = (exponent / jnp.sum(exponent, axis=-1, keepdims=True)).astype(jnp.bfloat16)
        attended = jnp.einsum(
            "gsqk,kgd->qgsd", weights, value_heads, preferred_element_type=jnp.float32
        )
        outputs_list.append(attended.reshape(longest, HEADS * HEAD_DIM).astype(jnp.bfloat16))
    stacked = jnp.concatenate(outputs_list, axis=0)
    gathered = stacked[request_of * longest + offset_in]
    projected = jnp.dot(gathered, w_out, preferred_element_type=jnp.float32)
    return (tokens_dev.astype(jnp.float32) + projected).astype(jnp.bfloat16)


MESH = pl.DeviceIdType.MESH
SIDE = 4
SLOTS = 32
HALF = 128
WIDTH = 1536
HIDDEN = 768
CHUNK = 2 * SIDE * SLOTS
PARTNERS = [
    (dz, dx, dy, dc)
    for dz in range(SIDE)
    for dx in range(SIDE)
    for dy in range(SIDE)
    for dc in range(2)
    if (dz == 0) + (dx == 0) + (dy == 0) >= 2 and (dz, dx, dy, dc) != (0, 0, 0, 0)
]


def place():
    row, column = lax.axis_index("dp"), lax.axis_index("expert")
    return row // SIDE, row % SIDE, column // 2, column % 2


def device_at(dz, dx, dy, dc):
    z, x, y, c = place()
    row = ((z + dz) % SIDE) * SIDE + (x + dx) % SIDE
    return (row, ((y + dy) % SIDE) * 2 + (c + dc) % 2)


def along(half, offset, dc=0):
    return device_at(half * offset, (1 - half) * offset, 0, dc)


def across(half, offset):
    return device_at((1 - half) * offset, half * offset, 0, 0)


def send(source, landing, sem_s, sem_r, device):
    return pltpu.make_async_remote_copy(
        src_ref=source,
        dst_ref=landing,
        send_sem=sem_s,
        recv_sem=sem_r,
        device_id=device,
        device_id_type=MESH,
    )


def moe_kernel(
    rows_ref,
    table_ref,
    counts_ref,
    residual_ref,
    gate_up_ref,
    down_ref,
    out_ref,
    owner_ref,
    held,
    tables,
    packed,
    landed,
    done,
    back_rows,
    partial,
    given,
    total,
    gate_up,
    down,
    tallies,
    told,
    s_first,
    r_first,
    s_table,
    r_table,
    s_out,
    r_out,
    s_back,
    r_back,
    s_give,
    r_give,
    s_tally,
    r_tally,
    s_weight,
    r_weight,
    s_pass,
    r_pass,
):
    z, x, y, c = place()
    barrier = pltpu.get_barrier_semaphore()
    for offsets in PARTNERS:
        pl.semaphore_signal(barrier, inc=1, device_id=device_at(*offsets), device_id_type=MESH)
    pl.semaphore_wait(barrier, len(PARTNERS))

    first = []
    for half in range(2):
        for back in (1, 3, 2):
            there = across(half, back)
            first.append(
                send(table_ref, tables.at[half, back], s_table.at[half, back], r_table.at[half, back], there)
            )
            first.append(
                send(
                    rows_ref.at[pl.ds(half * HALF, HALF)],
                    held.at[half, back],
                    s_first.at[half, back],
                    r_first.at[half, back],
                    there,
                )
            )
    for copy in first:
        copy.start()

    column = y * 2 + c
    shards = []
    for dc in range(2):
        expert = (c + dc) % 2
        for dy in (1, 3, 0):
            for kind, source, landing in (
                (0, gate_up_ref.at[expert], gate_up.at[:, column]),
                (1, down_ref.at[expert], down.at[column]),
            ):
                if dy == 0 and dc == 0:
                    copy = pltpu.make_async_copy(source, landing, r_weight.at[dy, dc, kind])
                else:
                    copy = send(
                        source,
                        landing,
                        s_weight.at[dy, dc, kind],
                        r_weight.at[dy, dc, kind],
                        device_at(0, 0, dy, dc),
                    )
                copy.start()
                shards.append(copy)

    tallies[0] = counts_ref[...]
    legs = [
        [(0, 1, 0, 0), (0, 2, 0, 0), (0, 3, 0, 0)],
        [(1, 0, 0, 0), (2, 0, 0, 0), (3, 0, 0, 0)],
        [(0, 0, 1, 0), (0, 0, 2, 0), (0, 0, 3, 0)],
        [(0, 0, 0, 1)],
    ]

    def tally(leg):
        copies = [
            send(tallies.at[leg], told.at[leg, k], s_tally.at[leg, k], r_tally.at[leg, k], device_at(*offsets))
            for k, offsets in enumerate(legs[leg])
        ]
        for copy in copies:
            copy.start()
        return copies

    def add_tallies(leg, copies):
        held_so_far = tallies[leg]
        for k, copy in enumerate(copies):
            copy.wait()
            held_so_far = held_so_far + told[leg, k]
        return held_so_far

    telling = tally(0)

    held[0, 0] = rows_ref[0:HALF, :]
    held[1, 0] = rows_ref[HALF : 2 * HALF, :]
    tables[0, 0] = table_ref[...]
    tables[1, 0] = table_ref[...]
    line = lax.broadcasted_iota(jnp.int32, (CHUNK, HALF), 0)

    def copies_out(half, back):
        at = (1 - half) * x + half * z
        copies = []
        for dc in (1, 0):
            for offset in (2, 1, 3, 0):
                piece = packed.at[half, back, (at + offset) % SIDE, (c + dc) % 2]
                landing = landed.at[half, back, offset, dc]
                arrival = r_out.at[half, back, offset, dc]
                if offset == 0 and dc == 0:
                    copies.append(pltpu.make_async_copy(piece, landing, arrival))
                else:
                    copies.append(
                        send(piece, landing, s_out.at[half, back, offset, dc], arrival, along(half, offset, dc))
                    )
        return copies

    def pack(half, back):
        if half == 0:
            wanted = line + z * CHUNK
        else:
            wanted = (line // 64) * CHUNK + x * 64 + line % 64
        table = tables[half, back]
        hot = jnp.zeros((CHUNK, HALF), jnp.bool_)
        for k in range(4):
            code = table[k : k + 1, half * HALF : (half + 1) * HALF].astype(jnp.int32)
            hot = hot | (code == wanted)
        spread = jnp.dot(
            hot.astype(jnp.float32).astype(jnp.bfloat16),
            held[half, back],
            preferred_element_type=jnp.float32,
        ).astype(jnp.bfloat16)
        packed[half, back] = spread.reshape(SIDE, 2, SLOTS, WIDTH)
        for copy in copies_out(half, back):
            copy.start()

    def arrive(half, back):
        send(table_ref, tables.at[half, back], s_table.at[half, back], r_table.at[half, back], across(half, back)).wait_recv()
        send(
            rows_ref.at[pl.ds(half * HALF, HALF)],
            held.at[half, back],
            s_first.at[half, back],
            r_first.at[half, back],
            across(half, back),
        ).wait_recv()

    for half in range(2):
        pack(half, 0)

    def pack_round(step, carry):
        back = 1 + (2 * step) % 3
        for half in range(2):
            arrive(half, back)
            pack(half, back)
        return carry

    lax.fori_loop(0, 3, pack_round, 0)

    passing = []
    for dc in range(2):
        for side, (dy, onward, low) in enumerate(((1, 1, 0), (3, 3, 1))):
            owner = ((y + SIDE - dy) % SIDE) * 2 + (c + dc) % 2
            for kind in range(2):
                if kind == 0:
                    whole, rows = gate_up.at[:, owner], 48
                    piece = gate_up.at[:, owner, pl.ds(low * rows, rows)]
                else:
                    whole, rows = down.at[owner], 96
                    piece = down.at[owner, pl.ds(low * rows, rows)]
                send(whole, whole, s_weight.at[dy, dc, kind], r_weight.at[dy, dc, kind], device_at(0, 0, dy, dc)).wait_recv()
                copy = send(
                    piece, piece, s_pass.at[side, dc, kind], r_pass.at[side, dc, kind], device_at(0, 0, onward, 0)
                )
                copy.start()
                passing.append(copy)

    for leg in range(1, 4):
        tallies[leg] = add_tallies(leg - 1, telling)
        telling = tally(leg)
    tallied = add_tallies(3, telling)
    me = lax.axis_index("dp") * 8 + lax.axis_index("expert")
    lane = lax.broadcasted_iota(jnp.int32, tallied.shape, 1)
    mine = jnp.sum(jnp.where(lane == me, tallied, 0).astype(jnp.float32), axis=1, keepdims=True)
    owner_ref[...] = jnp.broadcast_to(mine, tallied.shape).astype(jnp.int32)

    for kind in range(2):
        for dc in range(2):
            whole = gate_up.at[:, column] if kind == 0 else down.at[column]
            if dc == 0:
                source = gate_up_ref.at[c] if kind == 0 else down_ref.at[c]
                pltpu.make_async_copy(source, whole, r_weight.at[0, 0, kind]).wait()
            else:
                send(
                    whole, whole, s_weight.at[0, dc, kind], r_weight.at[0, dc, kind], device_at(0, 0, 0, 1)
                ).wait_recv()
    for copy in passing:
        copy.wait()

    def copies_back(half, back, own=True):
        copies = []
        for dc in (1, 0):
            for offset in (2, 1, 3, 0):
                if offset == 0 and dc == 0 and not own:
                    continue
                piece = done.at[half, back, offset, dc]
                landing = back_rows.at[half, back, offset, dc]
                arrival = r_back.at[half, back, offset, dc]
                if offset == 0 and dc == 0:
                    copies.append((pltpu.make_async_copy(piece, landing, arrival), False))
                else:
                    copies.append(
                        (
                            send(
                                piece,
                                landing,
                                s_back.at[half, back, offset, dc],
                                arrival,
                                along(half, SIDE - offset, dc),
                            ),
                            True,
                        )
                    )
        return copies

    last = (((1,), (1,)), ((), ()))

    def serve(step, carry):
        half, back = step % 2, (step // 2 + 1) % SIDE
        for copy in copies_out(half, back):
            copy.wait()
        arrived = landed[half, back].reshape(CHUNK, WIDTH)
        gate = lax.dot_general(
            arrived, gate_up[0].reshape(HIDDEN, WIDTH), last, preferred_element_type=jnp.float32
        )
        up = lax.dot_general(
            arrived, gate_up[1].reshape(HIDDEN, WIDTH), last, preferred_element_type=jnp.float32
        )
        hidden = (jnp.maximum(gate, 0.0) * up).astype(jnp.bfloat16)
        answer = lax.dot_general(
            hidden, down[...].reshape(WIDTH, HIDDEN), last, preferred_element_type=jnp.float32
        )
        done[half, back] = answer.astype(jnp.bfloat16).reshape(SIDE, 2, SLOTS, WIDTH)
        for copy, _ in copies_back(half, back):
            copy.start()
        return carry

    lax.fori_loop(0, 2 * SIDE, serve, 0)

    turn, swap, slot = line // 64, (line // 32) % 2, line % 32

    def mix(half, back):
        for copy, remote in copies_back(half, back):
            if remote:
                copy.wait_recv()
            else:
                copy.wait()
        if half == 0:
            owner = z * SIDE + (x + turn) % SIDE
        else:
            owner = ((z + turn) % SIDE) * SIDE + x
        wanted = owner * 64 + ((c + swap) % 2) * 32 + slot
        table = tables[half, back]
        weight = jnp.zeros((CHUNK, HALF), jnp.float32)
        for k in range(4):
            code = table[k : k + 1, half * HALF : (half + 1) * HALF].astype(jnp.int32)
            gate = table[4 + k : 5 + k, half * HALF : (half + 1) * HALF]
            weight = weight + jnp.where(code == wanted, gate, 0.0)
        coarse = weight.astype(jnp.bfloat16)
        fine = (weight - coarse.astype(jnp.float32)).astype(jnp.bfloat16)
        came = back_rows[half, back].reshape(CHUNK, WIDTH)
        rows = (((0,), (0,)), ((), ()))
        return lax.dot_general(
            coarse, came, rows, preferred_element_type=jnp.float32
        ) + lax.dot_general(fine, came, rows, preferred_element_type=jnp.float32)

    def gift(half, back):
        return send(
            partial.at[half, back],
            given.at[half, back],
            s_give.at[half, back],
            r_give.at[half, back],
            across(half, SIDE - back),
        )

    def mix_round(step, carry):
        for half in range(2):
            partial[half, step + 1] = mix(half, step + 1).astype(jnp.bfloat16)
            gift(half, step + 1).start()
        return carry

    lax.fori_loop(0, 3, mix_round, 0)
    for half in range(2):
        total[half] = mix(half, 0)
    for half in range(2):
        mixed = total[half]
        for back in (1, 2, 3):
            gift(half, back).wait_recv()
            mixed = mixed + given[half, back].astype(jnp.float32)
        here = pl.ds(half * HALF, HALF)
        out_ref[here, :] = (residual_ref[here, :].astype(jnp.float32) + mixed).astype(jnp.bfloat16)

    for copy in first:
        copy.wait_send()
    position = 0
    for dc in range(2):
        for dy in (1, 3, 0):
            for kind in range(2):
                if not (dy == 0 and dc == 0):
                    shards[position].wait_send()
                position += 1

    def settle(step, carry):
        half, back = step % 2, step // 2
        for copy, _ in copies_back(half, back, own=False):
            copy.wait_send()
        return carry

    lax.fori_loop(0, 2 * SIDE, settle, 0)
    for half in range(2):
        for back in (1, 2, 3):
            gift(half, back).wait_send()


def moe(rows, table, counts, residual, gate_up, down):
    any_space = pl.BlockSpec(memory_space=pl.ANY)
    vmem = pl.BlockSpec(memory_space=pltpu.VMEM)
    dma = pltpu.SemaphoreType.DMA
    chunks = (2, SIDE, SIDE, 2, SLOTS, WIDTH)
    halves = (2, SIDE, HALF, WIDTH)
    bf16 = jnp.bfloat16
    return pl.pallas_call(
        moe_kernel,
        out_shape=(
            jax.ShapeDtypeStruct((2 * HALF, WIDTH), bf16),
            jax.ShapeDtypeStruct((8, 128), jnp.int32),
        ),
        in_specs=[vmem, vmem, vmem, vmem, any_space, any_space],
        out_specs=(vmem, vmem),
        scratch_shapes=[
            pltpu.VMEM(halves, bf16),
            pltpu.VMEM((2, SIDE, 8, 2 * HALF), jnp.float32),
            pltpu.VMEM(chunks, bf16),
            pltpu.VMEM(chunks, bf16),
            pltpu.VMEM(chunks, bf16),
            pltpu.VMEM(chunks, bf16),
            pltpu.VMEM(halves, bf16),
            pltpu.VMEM(halves, bf16),
            pltpu.VMEM((2, HALF, WIDTH), jnp.float32),
            pltpu.VMEM((2, 8, 96, WIDTH), bf16),
            pltpu.VMEM((8, 192, HIDDEN), bf16),
            pltpu.VMEM((4, 8, 128), jnp.int32),
            pltpu.VMEM((4, 3, 8, 128), jnp.int32),
            dma((2, SIDE)),
            dma((2, SIDE)),
            dma((2, SIDE)),
            dma((2, SIDE)),
            dma((2, SIDE, SIDE, 2)),
            dma((2, SIDE, SIDE, 2)),
            dma((2, SIDE, SIDE, 2)),
            dma((2, SIDE, SIDE, 2)),
            dma((2, SIDE)),
            dma((2, SIDE)),
            dma((4, 3)),
            dma((4, 3)),
            dma((SIDE, 2, 2)),
            dma((SIDE, 2, 2)),
            dma((2, 2, 2)),
            dma((2, 2, 2)),
        ],
        name="moe",
        compiler_params=pltpu.CompilerParams(
            collective_id=1, has_side_effects=True, vmem_limit_bytes=60 << 20
        ),
        cost_estimate=pl.CostEstimate(flops=17 * 10**9, bytes_accessed=10**7, transcendentals=0),
    )(rows, table, counts, residual, gate_up, down)


def on_device(
    tokens,
    attn_gain,
    ffn_gain,
    w_query,
    w_key,
    w_value,
    w_out,
    key_cache,
    value_cache,
    req_lengths,
    cache_lengths,
    expert_ids,
    route_gate,
    replica_owner,
    replica_pick,
    w_gate_up,
    w_down,
):
    dp_count = lax.axis_size("dp")
    axis_count = lax.axis_size("expert")
    device_count = dp_count * axis_count
    local_experts = w_gate_up.shape[0]
    token_count = tokens.shape[0]
    expert_total = replica_owner.shape[0]
    sub_rows = token_count // axis_count

    experts = jnp.arange(expert_total, dtype=jnp.int32)
    route_hot = (expert_ids[:, :, None] == experts).astype(jnp.int32)
    blocked = jnp.sum(route_hot, axis=1).reshape(axis_count, sub_rows, expert_total)
    earlier = (
        jnp.arange(sub_rows, dtype=jnp.int32)[:, None] > jnp.arange(sub_rows, dtype=jnp.int32)[None, :]
    ).astype(jnp.bfloat16)
    before = jnp.einsum(
        "ts,bsx->btx", earlier, blocked.astype(jnp.bfloat16), preferred_element_type=jnp.float32
    ).reshape(token_count, 1, expert_total)
    rank = jnp.sum(route_hot.astype(jnp.float32) * before, axis=2)
    block_in_half = (jnp.arange(token_count, dtype=jnp.int32) // sub_rows) % 4
    codes = (expert_ids * SLOTS + block_in_half[:, None] * 8).astype(jnp.float32) + rank
    table = jnp.concatenate([codes.T, route_gate.T], axis=0)

    per_block = jnp.sum(blocked, axis=1)
    picked = (
        replica_pick[0][:, None] == jnp.arange(axis_count, dtype=jnp.int32)[None, :]
    ).astype(jnp.int32)
    owned = (
        replica_owner[:, :, None] == jnp.arange(axis_count, dtype=jnp.int32)[None, None, :]
    ).astype(jnp.int32)
    by_replica = jnp.sum(picked[:, None, :] * per_block[:, :, None], axis=0)
    by_owner = jnp.sum(by_replica[:, :, None] * owned, axis=1)
    counts = (
        by_owner.reshape(dp_count, local_experts, axis_count)
        .transpose(1, 0, 2)
        .reshape(local_experts, device_count)
    )
    counts = jnp.concatenate([counts, jnp.zeros((8 - local_experts, device_count), jnp.int32)], axis=0)

    residual = attend_device(
        tokens,
        req_lengths[0],
        cache_lengths[0],
        key_cache,
        value_cache,
        attn_gain,
        w_query,
        w_key,
        w_value,
        w_out,
    )
    normed_mid = rms_scale(residual, ffn_gain)
    layer_out, owner_counts = moe(
        normed_mid, table, counts, residual, w_gate_up.transpose(0, 2, 1, 3), w_down
    )
    return (layer_out, owner_counts[:local_experts, 0][None, :])


def solution(mesh):
    in_specs = (
        P(("dp", "expert"), None),
        P(),
        P(),
        P(),
        P(),
        P(),
        P(),
        P(("dp", "expert"), None, None),
        P(("dp", "expert"), None, None),
        P(("dp", "expert"), None),
        P(("dp", "expert"), None),
        P(("dp", "expert"), None),
        P(("dp", "expert"), None),
        P(),
        P(("dp", "expert"), None),
        P("dp", "expert", None, None),
        P("dp", "expert", None),
    )
    out_specs = (P(("dp", "expert"), None), P(("dp", "expert"), None))
    return jax.shard_map(
        on_device, mesh=mesh, in_specs=in_specs, out_specs=out_specs, check_vma=False
    )
```

```python
import jax
import jax.numpy as jnp
from jax import lax
from jax.experimental import pallas as pl
from jax.experimental.pallas import tpu as pltpu
from jax.sharding import PartitionSpec as P

HEADS = 12
KV_HEADS = 2
HEAD_DIM = 128


epsilon = 1e-06
rope_base = 1000000.0


GROUP = HEADS // KV_HEADS
TILE = 64
CACHE = 2048
OPEN = 1024


def front_kernel(
    lengths_ref,
    cached_ref,
    pick_ref,
    tokens_ref,
    attn_gain_ref,
    ffn_gain_ref,
    inverse_ref,
    ids_ref,
    gate_ref,
    owners_ref,
    w_query_hbm,
    w_key_hbm,
    w_value_hbm,
    w_out_hbm,
    keys_hbm,
    values_hbm,
    residual_ref,
    normed_ref,
    table_ref,
    counts_ref,
    w_query,
    w_key,
    w_value,
    w_out,
    keys,
    values,
    new_keys,
    new_values,
    queries,
    attended,
    sem_w,
    sem_k,
    sem_v,
):
    count = tokens_ref.shape[0]
    loads = [
        pltpu.make_async_copy(w_query_hbm, w_query, sem_w.at[0]),
        pltpu.make_async_copy(w_key_hbm, w_key, sem_w.at[1]),
        pltpu.make_async_copy(w_value_hbm, w_value, sem_w.at[2]),
    ]

    def cache_loads(request):
        copies = []
        for group in range(KV_HEADS):
            lanes = pl.ds(group * HEAD_DIM, HEAD_DIM)
            copies.append(
                pltpu.make_async_copy(
                    keys_hbm.at[request, :, lanes], keys.at[request, group], sem_k.at[request, group]
                )
            )
            copies.append(
                pltpu.make_async_copy(
                    values_hbm.at[request, :, lanes],
                    values.at[request, group, :, pl.ds(0, HEAD_DIM)],
                    sem_v.at[request, group],
                )
            )
        return copies

    last_load = pltpu.make_async_copy(w_out_hbm, w_out, sem_w.at[3])
    for copy in loads:
        copy.start()
    for request in range(3):
        for copy in cache_loads(request):
            copy.start()
    last_load.start()

    starts = [0, lengths_ref[0, 0], lengths_ref[0, 0] + lengths_ref[0, 1]]
    ends = [starts[1], starts[2], count]
    cached = [cached_ref[0, request] for request in range(3)]

    def by_request(token, values_of):
        return jnp.where(
            token < starts[1], values_of[0], jnp.where(token < starts[2], values_of[1], values_of[2])
        )

    lane = lax.broadcasted_iota(jnp.int32, (count, 128), 1)
    row = lax.broadcasted_iota(jnp.int32, (count, 128), 0)
    hots = [(ids_ref[:, k : k + 1] == lane).astype(jnp.float32) for k in range(4)]
    hot = hots[0] + hots[1] + hots[2] + hots[3]
    later = lax.broadcasted_iota(jnp.int32, (count, count), 0)
    sooner = lax.broadcasted_iota(jnp.int32, (count, count), 1)
    before = jnp.dot(
        ((later // 32 == sooner // 32) & (sooner < later)).astype(jnp.float32).astype(jnp.bfloat16),
        hot.astype(jnp.bfloat16),
        preferred_element_type=jnp.float32,
    )
    columns = jnp.zeros((count, 128), jnp.float32)
    for k in range(4):
        rank = jnp.sum(hots[k] * before, axis=1, keepdims=True)
        code = (ids_ref[:, k : k + 1] * 32).astype(jnp.float32) + rank
        columns = jnp.where(lane == k, code, columns)
        columns = jnp.where(lane == 4 + k, gate_ref[:, k : k + 1], columns)
    columns = columns + jnp.where(lane < 4, ((row // 32) % 4 * 8).astype(jnp.float32), 0.0)
    table_ref[...] = columns.T[0:8, :]

    blocks = lax.broadcasted_iota(jnp.int32, (8, count), 0)
    members = lax.broadcasted_iota(jnp.int32, (8, count), 1)
    per_block = jnp.dot(
        (members // 32 == blocks).astype(jnp.float32).astype(jnp.bfloat16),
        hot.astype(jnp.bfloat16),
        preferred_element_type=jnp.float32,
    )
    place_of = lax.broadcasted_iota(jnp.int32, (8, 128), 0)
    per_owner = jnp.zeros((8, 128), jnp.float32)
    for block in range(8):
        owner = owners_ref[pl.ds(pick_ref[0, block], 1), :]
        per_owner = per_owner + jnp.where(place_of == owner, per_block[block : block + 1, :], 0.0)
    expert_row = lax.broadcasted_iota(jnp.int32, (128, 128), 0)
    owner_lane = lax.broadcasted_iota(jnp.int32, (128, 128), 1)
    tallied = jnp.zeros((8, 128), jnp.float32)
    for j in range(2):
        moved = jnp.dot(
            per_owner.astype(jnp.bfloat16),
            (expert_row == owner_lane // 8 * 2 + j).astype(jnp.float32).astype(jnp.bfloat16),
            preferred_element_type=jnp.float32,
        )
        own = jnp.sum(
            jnp.where(lax.broadcasted_iota(jnp.int32, (8, 128), 1) % 8 == place_of, moved, 0.0),
            axis=0,
            keepdims=True,
        )
        tallied = jnp.where(place_of == j, own, tallied)
    counts_ref[...] = tallied.astype(jnp.int32)

    for request in range(3):
        for group in range(KV_HEADS):
            values[request, group, :, HEAD_DIM:] = jnp.ones((CACHE, HEAD_DIM), jnp.bfloat16)
    for group in range(KV_HEADS):
        new_values[group, :, HEAD_DIM:] = jnp.ones((count, HEAD_DIM), jnp.bfloat16)

    wide = tokens_ref[...].astype(jnp.float32)
    scale = lax.rsqrt(jnp.mean(wide * wide, axis=1, keepdims=True) + epsilon)
    normed = (wide * scale * attn_gain_ref[...]).astype(jnp.bfloat16)

    position = row + by_request(row, [cached[0], cached[1] - starts[1], cached[2] - starts[2]])
    angle = position.astype(jnp.float32) * inverse_ref[...]
    cosine = jnp.cos(angle)
    sine = jnp.sin(angle)
    sine = jnp.where(lane < HEAD_DIM // 2, -sine, sine)

    def turned(head):
        return (head * cosine + pltpu.roll(head, HEAD_DIM // 2, 1) * sine).astype(jnp.bfloat16)

    loads[0].wait()
    for part in range(HEADS // 2):
        pair = jnp.dot(
            normed,
            w_query[:, part * 256 : (part + 1) * 256],
            preferred_element_type=jnp.float32,
        )
        for side in range(2):
            queries[part * 2 + side] = turned(pair[:, side * HEAD_DIM : (side + 1) * HEAD_DIM])
    loads[1].wait()
    fresh_keys = jnp.dot(normed, w_key[...], preferred_element_type=jnp.float32)
    loads[2].wait()
    fresh_values = jnp.dot(normed, w_value[...], preferred_element_type=jnp.float32)
    for group in range(KV_HEADS):
        lanes = slice(group * HEAD_DIM, (group + 1) * HEAD_DIM)
        new_keys[group] = turned(fresh_keys[:, lanes])
        new_values[group, :, 0:HEAD_DIM] = fresh_values[:, lanes].astype(jnp.bfloat16)

    factor = HEAD_DIM ** (-0.5) * 1.4426950408889634
    stack = GROUP * TILE
    last = (((1,), (1,)), ((), ()))
    lowest = -jnp.inf
    for request in range(3):
        for copy in cache_loads(request):
            copy.wait()
        start, end, filled = starts[request], ends[request], cached[request]

        def attend(tile, carry, request=request, start=start, end=end, filled=filled):
            base = pl.multiple_of(tile * TILE, TILE)
            token = base + lax.broadcasted_iota(jnp.int32, (stack, 128), 0) % TILE
            here = filled + token - start
            slot = lax.broadcasted_iota(jnp.int32, (stack, 128), 1)
            near = (slot == 0) | (here - slot < CACHE)
            open_slot = OPEN + lax.broadcasted_iota(jnp.int32, (1, CACHE - OPEN), 1)
            bias = jnp.where(open_slot < filled, 0.0, lowest)
            fresh = lax.broadcasted_iota(jnp.int32, (stack, count), 1)
            asking = base + lax.broadcasted_iota(jnp.int32, (stack, count), 0) % TILE
            seen = (fresh >= start) & (fresh <= asking)
            inside = (token >= start) & (token < end)
            for group in range(KV_HEADS):
                asked = queries[group * GROUP : (group + 1) * GROUP, pl.ds(base, TILE), :].reshape(
                    stack, HEAD_DIM
                )

                def score(block):
                    return lax.dot_general(asked, block, last, preferred_element_type=jnp.float32)

                parts = [
                    jnp.where(near, score(keys[request, group, 0:128, :]), lowest),
                    score(keys[request, group, 128:OPEN, :]),
                    score(keys[request, group, OPEN:CACHE, :]) + bias,
                    jnp.where(seen, score(new_keys[group]), lowest),
                ]
                peak = jnp.max(parts[0], axis=1, keepdims=True)
                for part in parts[1:]:
                    peak = jnp.maximum(peak, jnp.max(part, axis=1, keepdims=True))
                peak = peak * factor
                blocks = [
                    values[request, group, 0:128, :],
                    values[request, group, 128:OPEN, :],
                    values[request, group, OPEN:CACHE, :],
                    new_values[group],
                ]
                mixed = jnp.zeros((stack, 2 * HEAD_DIM), jnp.float32)
                for part, block in zip(parts, blocks):
                    weight = jnp.exp2(part * factor - peak).astype(jnp.bfloat16)
                    mixed = mixed + jnp.dot(weight, block, preferred_element_type=jnp.float32)
                answer = mixed[:, 0:HEAD_DIM] / mixed[:, HEAD_DIM:]
                for member in range(GROUP):
                    rows = slice(member * TILE, (member + 1) * TILE)
                    head = group * GROUP + member
                    spot = (pl.ds(base, TILE), slice(head * HEAD_DIM, (head + 1) * HEAD_DIM))
                    kept = attended[spot].astype(jnp.float32)
                    attended[spot] = jnp.where(inside[rows], answer[rows], kept).astype(jnp.bfloat16)
            return carry

        lax.fori_loop(start // TILE, (end + TILE - 1) // TILE, attend, 0)

    last_load.wait()
    projected = jnp.dot(attended[...], w_out[...], preferred_element_type=jnp.float32)
    residual = (tokens_ref[...].astype(jnp.float32) + projected).astype(jnp.bfloat16)
    residual_ref[...] = residual
    wide = residual.astype(jnp.float32)
    scale = lax.rsqrt(jnp.mean(wide * wide, axis=1, keepdims=True) + epsilon)
    normed_ref[...] = (wide * scale * ffn_gain_ref[...]).astype(jnp.bfloat16)


def front(
    tokens,
    attn_gain,
    ffn_gain,
    w_query,
    w_key,
    w_value,
    w_out,
    key_cache,
    value_cache,
    lengths,
    cached,
    pick,
    ids,
    gates,
    replica_owner,
):
    count, width = tokens.shape
    any_space = pl.BlockSpec(memory_space=pl.ANY)
    vmem = pl.BlockSpec(memory_space=pltpu.VMEM)
    smem = pl.BlockSpec(memory_space=pltpu.SMEM)
    dma = pltpu.SemaphoreType.DMA
    bf16 = jnp.bfloat16
    half_dim = HEAD_DIM // 2
    inverse = rope_base ** (-(jnp.arange(half_dim, dtype=jnp.float32) * 2.0 / HEAD_DIM))
    inverse = jnp.concatenate([inverse, inverse])[None, :]
    owners = jnp.pad(replica_owner.T, ((0, 0), (0, 128 - replica_owner.shape[0])))
    return pl.pallas_call(
        front_kernel,
        out_shape=(
            jax.ShapeDtypeStruct((count, width), bf16),
            jax.ShapeDtypeStruct((count, width), bf16),
            jax.ShapeDtypeStruct((8, count), jnp.float32),
            jax.ShapeDtypeStruct((8, 128), jnp.int32),
        ),
        in_specs=[smem] * 3 + [vmem] * 7 + [any_space] * 6,
        out_specs=(vmem,) * 4,
        scratch_shapes=[
            pltpu.VMEM(w_query.shape, bf16),
            pltpu.VMEM(w_key.shape, bf16),
            pltpu.VMEM(w_value.shape, bf16),
            pltpu.VMEM(w_out.shape, bf16),
            pltpu.VMEM((3, KV_HEADS, CACHE, HEAD_DIM), bf16),
            pltpu.VMEM((3, KV_HEADS, CACHE, 2 * HEAD_DIM), bf16),
            pltpu.VMEM((KV_HEADS, count, HEAD_DIM), bf16),
            pltpu.VMEM((KV_HEADS, count, 2 * HEAD_DIM), bf16),
            pltpu.VMEM((HEADS, count, HEAD_DIM), bf16),
            pltpu.VMEM((count, HEADS * HEAD_DIM), bf16),
            dma((4,)),
            dma((3, KV_HEADS)),
            dma((3, KV_HEADS)),
        ],
        name="front",
        compiler_params=pltpu.CompilerParams(vmem_limit_bytes=58 << 20),
    )(
        lengths,
        cached,
        pick,
        tokens,
        attn_gain[None, :],
        ffn_gain[None, :],
        inverse,
        ids,
        gates,
        owners,
        w_query,
        w_key,
        w_value,
        w_out,
        key_cache,
        value_cache,
    )


MESH = pl.DeviceIdType.MESH
SIDE = 4
SLOTS = 32
HALF = 128
WIDTH = 1536
HIDDEN = 768
CHUNK = 2 * SIDE * SLOTS
PARTNERS = [
    (dz, dx, dy, dc)
    for dz in range(SIDE)
    for dx in range(SIDE)
    for dy in range(SIDE)
    for dc in range(2)
    if (dz == 0) + (dx == 0) + (dy == 0) >= 2 and (dz, dx, dy, dc) != (0, 0, 0, 0)
]


def place():
    row, column = lax.axis_index("dp"), lax.axis_index("expert")
    return row // SIDE, row % SIDE, column // 2, column % 2


def device_at(dz, dx, dy, dc):
    z, x, y, c = place()
    row = ((z + dz) % SIDE) * SIDE + (x + dx) % SIDE
    return (row, ((y + dy) % SIDE) * 2 + (c + dc) % 2)


def along(half, offset, dc=0):
    return device_at(half * offset, (1 - half) * offset, 0, dc)


def across(half, offset):
    return device_at((1 - half) * offset, half * offset, 0, 0)


def send(source, landing, sem_s, sem_r, device):
    return pltpu.make_async_remote_copy(
        src_ref=source,
        dst_ref=landing,
        send_sem=sem_s,
        recv_sem=sem_r,
        device_id=device,
        device_id_type=MESH,
    )


def moe_kernel(
    rows_ref,
    table_ref,
    counts_ref,
    residual_ref,
    gate_up_ref,
    down_ref,
    out_ref,
    owner_ref,
    held,
    tables,
    packed,
    landed,
    done,
    back_rows,
    partial,
    given,
    total,
    gate_up,
    down,
    tallies,
    told,
    s_first,
    r_first,
    s_table,
    r_table,
    s_out,
    r_out,
    s_back,
    r_back,
    s_give,
    r_give,
    s_tally,
    r_tally,
    s_weight,
    r_weight,
    s_pass,
    r_pass,
):
    z, x, y, c = place()
    barrier = pltpu.get_barrier_semaphore()
    for offsets in PARTNERS:
        pl.semaphore_signal(barrier, inc=1, device_id=device_at(*offsets), device_id_type=MESH)
    pl.semaphore_wait(barrier, len(PARTNERS))

    first = []
    for half in range(2):
        for back in (1, 3, 2):
            there = across(half, back)
            first.append(
                send(table_ref, tables.at[half, back], s_table.at[half, back], r_table.at[half, back], there)
            )
            first.append(
                send(
                    rows_ref.at[pl.ds(half * HALF, HALF)],
                    held.at[half, back],
                    s_first.at[half, back],
                    r_first.at[half, back],
                    there,
                )
            )
    for copy in first:
        copy.start()

    column = y * 2 + c
    shards = []
    for dc in range(2):
        expert = (c + dc) % 2
        for dy in (1, 3, 0):
            for kind, source, landing in (
                (0, gate_up_ref.at[expert], gate_up.at[:, column]),
                (1, down_ref.at[expert], down.at[column]),
            ):
                if dy == 0 and dc == 0:
                    copy = pltpu.make_async_copy(source, landing, r_weight.at[dy, dc, kind])
                else:
                    copy = send(
                        source,
                        landing,
                        s_weight.at[dy, dc, kind],
                        r_weight.at[dy, dc, kind],
                        device_at(0, 0, dy, dc),
                    )
                copy.start()
                shards.append(copy)

    tallies[0] = counts_ref[...]
    legs = [
        [(0, 1, 0, 0), (0, 2, 0, 0), (0, 3, 0, 0)],
        [(1, 0, 0, 0), (2, 0, 0, 0), (3, 0, 0, 0)],
        [(0, 0, 1, 0), (0, 0, 2, 0), (0, 0, 3, 0)],
        [(0, 0, 0, 1)],
    ]

    def tally(leg):
        copies = [
            send(tallies.at[leg], told.at[leg, k], s_tally.at[leg, k], r_tally.at[leg, k], device_at(*offsets))
            for k, offsets in enumerate(legs[leg])
        ]
        for copy in copies:
            copy.start()
        return copies

    def add_tallies(leg, copies):
        held_so_far = tallies[leg]
        for k, copy in enumerate(copies):
            copy.wait()
            held_so_far = held_so_far + told[leg, k]
        return held_so_far

    telling = tally(0)

    held[0, 0] = rows_ref[0:HALF, :]
    held[1, 0] = rows_ref[HALF : 2 * HALF, :]
    tables[0, 0] = table_ref[...]
    tables[1, 0] = table_ref[...]
    line = lax.broadcasted_iota(jnp.int32, (CHUNK, HALF), 0)

    def copies_out(half, back):
        at = (1 - half) * x + half * z
        copies = []
        for dc in (1, 0):
            for offset in (2, 1, 3, 0):
                piece = packed.at[half, back, (at + offset) % SIDE, (c + dc) % 2]
                landing = landed.at[half, back, offset, dc]
                arrival = r_out.at[half, back, offset, dc]
                if offset == 0 and dc == 0:
                    copies.append(pltpu.make_async_copy(piece, landing, arrival))
                else:
                    copies.append(
                        send(piece, landing, s_out.at[half, back, offset, dc], arrival, along(half, offset, dc))
                    )
        return copies

    def pack(half, back):
        if half == 0:
            wanted = line + z * CHUNK
        else:
            wanted = (line // 64) * CHUNK + x * 64 + line % 64
        table = tables[half, back]
        hot = jnp.zeros((CHUNK, HALF), jnp.bool_)
        for k in range(4):
            code = table[k : k + 1, half * HALF : (half + 1) * HALF].astype(jnp.int32)
            hot = hot | (code == wanted)
        spread = jnp.dot(
            hot.astype(jnp.float32).astype(jnp.bfloat16),
            held[half, back],
            preferred_element_type=jnp.float32,
        ).astype(jnp.bfloat16)
        packed[half, back] = spread.reshape(SIDE, 2, SLOTS, WIDTH)
        for copy in copies_out(half, back):
            copy.start()

    def arrive(half, back):
        send(table_ref, tables.at[half, back], s_table.at[half, back], r_table.at[half, back], across(half, back)).wait_recv()
        send(
            rows_ref.at[pl.ds(half * HALF, HALF)],
            held.at[half, back],
            s_first.at[half, back],
            r_first.at[half, back],
            across(half, back),
        ).wait_recv()

    for half in range(2):
        pack(half, 0)

    def pack_round(step, carry):
        back = 1 + (2 * step) % 3
        for half in range(2):
            arrive(half, back)
            pack(half, back)
        return carry

    lax.fori_loop(0, 3, pack_round, 0)

    passing = []
    for dc in range(2):
        for side, (dy, onward, low) in enumerate(((1, 1, 0), (3, 3, 1))):
            owner = ((y + SIDE - dy) % SIDE) * 2 + (c + dc) % 2
            for kind in range(2):
                if kind == 0:
                    whole, rows = gate_up.at[:, owner], 48
                    piece = gate_up.at[:, owner, pl.ds(low * rows, rows)]
                else:
                    whole, rows = down.at[owner], 96
                    piece = down.at[owner, pl.ds(low * rows, rows)]
                send(whole, whole, s_weight.at[dy, dc, kind], r_weight.at[dy, dc, kind], device_at(0, 0, dy, dc)).wait_recv()
                copy = send(
                    piece, piece, s_pass.at[side, dc, kind], r_pass.at[side, dc, kind], device_at(0, 0, onward, 0)
                )
                copy.start()
                passing.append(copy)

    for leg in range(1, 4):
        tallies[leg] = add_tallies(leg - 1, telling)
        telling = tally(leg)
    tallied = add_tallies(3, telling)
    me = lax.axis_index("dp") * 8 + lax.axis_index("expert")
    lane = lax.broadcasted_iota(jnp.int32, tallied.shape, 1)
    mine = jnp.sum(jnp.where(lane == me, tallied, 0).astype(jnp.float32), axis=1, keepdims=True)
    owner_ref[...] = jnp.broadcast_to(mine, tallied.shape).astype(jnp.int32)

    for kind in range(2):
        for dc in range(2):
            whole = gate_up.at[:, column] if kind == 0 else down.at[column]
            if dc == 0:
                source = gate_up_ref.at[c] if kind == 0 else down_ref.at[c]
                pltpu.make_async_copy(source, whole, r_weight.at[0, 0, kind]).wait()
            else:
                send(
                    whole, whole, s_weight.at[0, dc, kind], r_weight.at[0, dc, kind], device_at(0, 0, 0, 1)
                ).wait_recv()
    for copy in passing:
        copy.wait()

    def copies_back(half, back, own=True):
        copies = []
        for dc in (1, 0):
            for offset in (2, 1, 3, 0):
                if offset == 0 and dc == 0 and not own:
                    continue
                piece = done.at[half, back, offset, dc]
                landing = back_rows.at[half, back, offset, dc]
                arrival = r_back.at[half, back, offset, dc]
                if offset == 0 and dc == 0:
                    copies.append((pltpu.make_async_copy(piece, landing, arrival), False))
                else:
                    copies.append(
                        (
                            send(
                                piece,
                                landing,
                                s_back.at[half, back, offset, dc],
                                arrival,
                                along(half, SIDE - offset, dc),
                            ),
                            True,
                        )
                    )
        return copies

    last = (((1,), (1,)), ((), ()))

    def serve(step, carry):
        half, back = step % 2, (step // 2 + 1) % SIDE
        for copy in copies_out(half, back):
            copy.wait()
        arrived = landed[half, back].reshape(CHUNK, WIDTH)
        gate = lax.dot_general(
            arrived, gate_up[0].reshape(HIDDEN, WIDTH), last, preferred_element_type=jnp.float32
        )
        up = lax.dot_general(
            arrived, gate_up[1].reshape(HIDDEN, WIDTH), last, preferred_element_type=jnp.float32
        )
        hidden = (jnp.maximum(gate, 0.0) * up).astype(jnp.bfloat16)
        answer = lax.dot_general(
            hidden, down[...].reshape(WIDTH, HIDDEN), last, preferred_element_type=jnp.float32
        )
        done[half, back] = answer.astype(jnp.bfloat16).reshape(SIDE, 2, SLOTS, WIDTH)
        for copy, _ in copies_back(half, back):
            copy.start()
        return carry

    lax.fori_loop(0, 2 * SIDE, serve, 0)

    turn, swap, slot = line // 64, (line // 32) % 2, line % 32

    def mix(half, back):
        for copy, remote in copies_back(half, back):
            if remote:
                copy.wait_recv()
            else:
                copy.wait()
        if half == 0:
            owner = z * SIDE + (x + turn) % SIDE
        else:
            owner = ((z + turn) % SIDE) * SIDE + x
        wanted = owner * 64 + ((c + swap) % 2) * 32 + slot
        table = tables[half, back]
        weight = jnp.zeros((CHUNK, HALF), jnp.float32)
        for k in range(4):
            code = table[k : k + 1, half * HALF : (half + 1) * HALF].astype(jnp.int32)
            gate = table[4 + k : 5 + k, half * HALF : (half + 1) * HALF]
            weight = weight + jnp.where(code == wanted, gate, 0.0)
        coarse = weight.astype(jnp.bfloat16)
        fine = (weight - coarse.astype(jnp.float32)).astype(jnp.bfloat16)
        came = back_rows[half, back].reshape(CHUNK, WIDTH)
        rows = (((0,), (0,)), ((), ()))
        return lax.dot_general(
            coarse, came, rows, preferred_element_type=jnp.float32
        ) + lax.dot_general(fine, came, rows, preferred_element_type=jnp.float32)

    def gift(half, back):
        return send(
            partial.at[half, back],
            given.at[half, back],
            s_give.at[half, back],
            r_give.at[half, back],
            across(half, SIDE - back),
        )

    def mix_round(step, carry):
        for half in range(2):
            partial[half, step + 1] = mix(half, step + 1).astype(jnp.bfloat16)
            gift(half, step + 1).start()
        return carry

    lax.fori_loop(0, 3, mix_round, 0)
    for half in range(2):
        total[half] = mix(half, 0)
    for half in range(2):
        mixed = total[half]
        for back in (1, 2, 3):
            gift(half, back).wait_recv()
            mixed = mixed + given[half, back].astype(jnp.float32)
        here = pl.ds(half * HALF, HALF)
        out_ref[here, :] = (residual_ref[here, :].astype(jnp.float32) + mixed).astype(jnp.bfloat16)

    for copy in first:
        copy.wait_send()
    position = 0
    for dc in range(2):
        for dy in (1, 3, 0):
            for kind in range(2):
                if not (dy == 0 and dc == 0):
                    shards[position].wait_send()
                position += 1

    def settle(step, carry):
        half, back = step % 2, step // 2
        for copy, _ in copies_back(half, back, own=False):
            copy.wait_send()
        return carry

    lax.fori_loop(0, 2 * SIDE, settle, 0)
    for half in range(2):
        for back in (1, 2, 3):
            gift(half, back).wait_send()


def moe(rows, table, counts, residual, gate_up, down):
    any_space = pl.BlockSpec(memory_space=pl.ANY)
    vmem = pl.BlockSpec(memory_space=pltpu.VMEM)
    dma = pltpu.SemaphoreType.DMA
    chunks = (2, SIDE, SIDE, 2, SLOTS, WIDTH)
    halves = (2, SIDE, HALF, WIDTH)
    bf16 = jnp.bfloat16
    return pl.pallas_call(
        moe_kernel,
        out_shape=(
            jax.ShapeDtypeStruct((2 * HALF, WIDTH), bf16),
            jax.ShapeDtypeStruct((8, 128), jnp.int32),
        ),
        in_specs=[vmem, vmem, vmem, vmem, any_space, any_space],
        out_specs=(vmem, vmem),
        scratch_shapes=[
            pltpu.VMEM(halves, bf16),
            pltpu.VMEM((2, SIDE, 8, 2 * HALF), jnp.float32),
            pltpu.VMEM(chunks, bf16),
            pltpu.VMEM(chunks, bf16),
            pltpu.VMEM(chunks, bf16),
            pltpu.VMEM(chunks, bf16),
            pltpu.VMEM(halves, bf16),
            pltpu.VMEM(halves, bf16),
            pltpu.VMEM((2, HALF, WIDTH), jnp.float32),
            pltpu.VMEM((2, 8, 96, WIDTH), bf16),
            pltpu.VMEM((8, 192, HIDDEN), bf16),
            pltpu.VMEM((4, 8, 128), jnp.int32),
            pltpu.VMEM((4, 3, 8, 128), jnp.int32),
            dma((2, SIDE)),
            dma((2, SIDE)),
            dma((2, SIDE)),
            dma((2, SIDE)),
            dma((2, SIDE, SIDE, 2)),
            dma((2, SIDE, SIDE, 2)),
            dma((2, SIDE, SIDE, 2)),
            dma((2, SIDE, SIDE, 2)),
            dma((2, SIDE)),
            dma((2, SIDE)),
            dma((4, 3)),
            dma((4, 3)),
            dma((SIDE, 2, 2)),
            dma((SIDE, 2, 2)),
            dma((2, 2, 2)),
            dma((2, 2, 2)),
        ],
        name="moe",
        compiler_params=pltpu.CompilerParams(
            collective_id=1, has_side_effects=True, vmem_limit_bytes=60 << 20
        ),
        cost_estimate=pl.CostEstimate(flops=17 * 10**9, bytes_accessed=10**7, transcendentals=0),
    )(rows, table, counts, residual, gate_up, down)


def on_device(
    tokens,
    attn_gain,
    ffn_gain,
    w_query,
    w_key,
    w_value,
    w_out,
    key_cache,
    value_cache,
    req_lengths,
    cache_lengths,
    expert_ids,
    route_gate,
    replica_owner,
    replica_pick,
    w_gate_up,
    w_down,
):
    residual, normed_mid, table, counts = front(
        tokens,
        attn_gain,
        ffn_gain,
        w_query,
        w_key,
        w_value,
        w_out,
        key_cache,
        value_cache,
        req_lengths,
        cache_lengths,
        replica_pick,
        expert_ids,
        route_gate,
        replica_owner,
    )
    layer_out, owner_counts = moe(
        normed_mid, table, counts, residual, w_gate_up.transpose(0, 2, 1, 3), w_down
    )
    return (layer_out, owner_counts[: w_gate_up.shape[0], 0][None, :])


def solution(mesh):
    in_specs = (
        P(("dp", "expert"), None),
        P(),
        P(),
        P(),
        P(),
        P(),
        P(),
        P(("dp", "expert"), None, None),
        P(("dp", "expert"), None, None),
        P(("dp", "expert"), None),
        P(("dp", "expert"), None),
        P(("dp", "expert"), None),
        P(("dp", "expert"), None),
        P(),
        P(("dp", "expert"), None),
        P("dp", "expert", None, None),
        P("dp", "expert", None),
    )
    out_specs = (P(("dp", "expert"), None), P(("dp", "expert"), None))
    return jax.shard_map(
        on_device, mesh=mesh, in_specs=in_specs, out_specs=out_specs, check_vma=False
    )
```

```python
import jax
import jax.numpy as jnp
import numpy as np
from jax import lax
from jax.experimental import pallas as pl
from jax.experimental.pallas import tpu as pltpu
from jax.sharding import PartitionSpec as P

HEADS = 12
KV_HEADS = 2
HEAD_DIM = 128


epsilon = 1e-06
rope_base = 1000000.0


GROUP = HEADS // KV_HEADS
TILE = 64
CACHE = 2048
OPEN = 1024


def front_kernel(
    lengths_ref,
    cached_ref,
    pick_ref,
    tokens_ref,
    attn_gain_ref,
    ffn_gain_ref,
    inverse_ref,
    ids_ref,
    gate_ref,
    owners_ref,
    w_query_hbm,
    w_key_hbm,
    w_value_hbm,
    w_out_hbm,
    keys_hbm,
    values_hbm,
    residual_ref,
    normed_ref,
    table_ref,
    counts_ref,
    w_query,
    w_key,
    w_value,
    w_out,
    keys,
    values,
    new_keys,
    new_values,
    queries,
    attended,
    sem_w,
    sem_k,
    sem_v,
):
    count = tokens_ref.shape[0]
    loads = [
        pltpu.make_async_copy(w_query_hbm, w_query, sem_w.at[0]),
        pltpu.make_async_copy(w_key_hbm, w_key, sem_w.at[1]),
        pltpu.make_async_copy(w_value_hbm, w_value, sem_w.at[2]),
    ]

    def cache_loads(request):
        copies = []
        for group in range(KV_HEADS):
            lanes = pl.ds(group * HEAD_DIM, HEAD_DIM)
            copies.append(
                pltpu.make_async_copy(
                    keys_hbm.at[request, :, lanes], keys.at[request, group], sem_k.at[request, group]
                )
            )
            copies.append(
                pltpu.make_async_copy(
                    values_hbm.at[request, :, lanes],
                    values.at[request, group, :, pl.ds(0, HEAD_DIM)],
                    sem_v.at[request, group],
                )
            )
        return copies

    last_load = pltpu.make_async_copy(w_out_hbm, w_out, sem_w.at[3])
    for copy in loads:
        copy.start()
    for request in range(3):
        for copy in cache_loads(request):
            copy.start()
    last_load.start()

    starts = [0, lengths_ref[0, 0], lengths_ref[0, 0] + lengths_ref[0, 1]]
    ends = [starts[1], starts[2], count]
    cached = [cached_ref[0, request] for request in range(3)]

    def by_request(token, values_of):
        return jnp.where(
            token < starts[1], values_of[0], jnp.where(token < starts[2], values_of[1], values_of[2])
        )

    lane = lax.broadcasted_iota(jnp.int32, (count, 128), 1)
    row = lax.broadcasted_iota(jnp.int32, (count, 128), 0)
    expert = lax.broadcasted_iota(jnp.int32, (32, count), 0)
    ids = [ids_ref[k : k + 1, :] for k in range(4)]
    hots = [(ids[k] == expert).astype(jnp.float32) for k in range(4)]
    hot = (hots[0] + hots[1] + hots[2] + hots[3]).astype(jnp.bfloat16)
    sooner = lax.broadcasted_iota(jnp.int32, (count, count), 0)
    later = lax.broadcasted_iota(jnp.int32, (count, count), 1)
    before = jnp.dot(
        hot,
        ((later // 32 == sooner // 32) & (sooner < later)).astype(jnp.float32).astype(jnp.bfloat16),
        preferred_element_type=jnp.float32,
    )
    line = lax.broadcasted_iota(jnp.int32, (8, count), 0)
    offset = lax.broadcasted_iota(jnp.int32, (1, count), 1) // 32 % 4 * 8
    table = jnp.zeros((8, count), jnp.float32)
    for k in range(4):
        rank = jnp.sum(hots[k] * before, axis=0, keepdims=True)
        code = (ids[k] * 32 + offset).astype(jnp.float32) + rank
        table = jnp.where(line == k, code, table)
        table = jnp.where(line == 4 + k, gate_ref[k : k + 1, :], table)
    table_ref[...] = table

    members = lax.broadcasted_iota(jnp.int32, (8, count), 1)
    last = (((1,), (1,)), ((), ()))
    per_block = lax.dot_general(
        (members // 32 == line).astype(jnp.float32).astype(jnp.bfloat16),
        hot,
        last,
        preferred_element_type=jnp.float32,
    )
    place_of = lax.broadcasted_iota(jnp.int32, (8, 32), 0)
    per_owner = jnp.zeros((8, 32), jnp.float32)
    for block in range(8):
        owner = owners_ref[pl.ds(pick_ref[0, block], 1), :]
        per_owner = per_owner + jnp.where(place_of == owner, per_block[block : block + 1, :], 0.0)
    expert_row = lax.broadcasted_iota(jnp.int32, (32, 128), 0)
    owner_lane = lax.broadcasted_iota(jnp.int32, (32, 128), 1)
    own_line = lax.broadcasted_iota(jnp.int32, (8, 128), 0)
    own_lane = lax.broadcasted_iota(jnp.int32, (8, 128), 1)
    tallied = jnp.zeros((8, 128), jnp.float32)
    for j in range(2):
        moved = jnp.dot(
            per_owner.astype(jnp.bfloat16),
            (expert_row == owner_lane // 8 * 2 + j).astype(jnp.float32).astype(jnp.bfloat16),
            preferred_element_type=jnp.float32,
        )
        own = jnp.sum(jnp.where(own_lane % 8 == own_line, moved, 0.0), axis=0, keepdims=True)
        tallied = jnp.where(own_line == j, own, tallied)
    counts_ref[...] = tallied.astype(jnp.int32)

    for request in range(3):
        for group in range(KV_HEADS):
            values[request, group, :, HEAD_DIM:] = jnp.ones((CACHE, HEAD_DIM), jnp.bfloat16)
    for group in range(KV_HEADS):
        new_values[group, :, HEAD_DIM:] = jnp.ones((count, HEAD_DIM), jnp.bfloat16)

    wide = tokens_ref[...].astype(jnp.float32)
    scale = lax.rsqrt(jnp.mean(wide * wide, axis=1, keepdims=True) + epsilon)
    normed = (wide * scale * attn_gain_ref[...].reshape(1, -1)).astype(jnp.bfloat16)

    position = row + by_request(row, [cached[0], cached[1] - starts[1], cached[2] - starts[2]])
    angle = position.astype(jnp.float32) * inverse_ref[...]
    cosine = jnp.cos(angle)
    sine = jnp.sin(angle)
    sine = jnp.where(lane < HEAD_DIM // 2, -sine, sine)

    def turned(head):
        return (head * cosine + pltpu.roll(head, HEAD_DIM // 2, 1) * sine).astype(jnp.bfloat16)

    loads[0].wait()
    for part in range(HEADS // 2):
        pair = jnp.dot(
            normed,
            w_query[:, part * 256 : (part + 1) * 256],
            preferred_element_type=jnp.float32,
        )
        for side in range(2):
            queries[part * 2 + side] = turned(pair[:, side * HEAD_DIM : (side + 1) * HEAD_DIM])
    loads[1].wait()
    fresh_keys = jnp.dot(normed, w_key[...], preferred_element_type=jnp.float32)
    loads[2].wait()
    fresh_values = jnp.dot(normed, w_value[...], preferred_element_type=jnp.float32)
    for group in range(KV_HEADS):
        lanes = slice(group * HEAD_DIM, (group + 1) * HEAD_DIM)
        new_keys[group] = turned(fresh_keys[:, lanes])
        new_values[group, :, 0:HEAD_DIM] = fresh_values[:, lanes].astype(jnp.bfloat16)

    factor = HEAD_DIM ** (-0.5) * 1.4426950408889634
    stack = GROUP * TILE
    lowest = -jnp.inf
    for request in range(3):
        for copy in cache_loads(request):
            copy.wait()
        start, end, filled = starts[request], ends[request], cached[request]

        def attend(tile, carry, request=request, start=start, end=end, filled=filled):
            base = pl.multiple_of(tile * TILE, TILE)
            token = base + lax.broadcasted_iota(jnp.int32, (stack, 128), 0) % TILE
            here = filled + token - start
            slot = lax.broadcasted_iota(jnp.int32, (stack, 128), 1)
            near = (slot == 0) | (here - slot < CACHE)
            open_slot = OPEN + lax.broadcasted_iota(jnp.int32, (1, CACHE - OPEN), 1)
            bias = jnp.where(open_slot < filled, 0.0, lowest)
            fresh = lax.broadcasted_iota(jnp.int32, (stack, count), 1)
            asking = base + lax.broadcasted_iota(jnp.int32, (stack, count), 0) % TILE
            seen = (fresh >= start) & (fresh <= asking)
            inside = (token >= start) & (token < end)
            for group in range(KV_HEADS):
                asked = queries[group * GROUP : (group + 1) * GROUP, pl.ds(base, TILE), :].reshape(
                    stack, HEAD_DIM
                )

                def score(block):
                    return lax.dot_general(asked, block, last, preferred_element_type=jnp.float32)

                parts = [
                    jnp.where(near, score(keys[request, group, 0:128, :]), lowest),
                    score(keys[request, group, 128:OPEN, :]),
                    score(keys[request, group, OPEN:CACHE, :]) + bias,
                    jnp.where(seen, score(new_keys[group]), lowest),
                ]
                peak = jnp.max(parts[0], axis=1, keepdims=True)
                for part in parts[1:]:
                    peak = jnp.maximum(peak, jnp.max(part, axis=1, keepdims=True))
                peak = peak * factor
                blocks = [
                    values[request, group, 0:128, :],
                    values[request, group, 128:OPEN, :],
                    values[request, group, OPEN:CACHE, :],
                    new_values[group],
                ]
                mixed = jnp.zeros((stack, 2 * HEAD_DIM), jnp.float32)
                for part, block in zip(parts, blocks):
                    weight = jnp.exp2(part * factor - peak).astype(jnp.bfloat16)
                    mixed = mixed + jnp.dot(weight, block, preferred_element_type=jnp.float32)
                answer = mixed[:, 0:HEAD_DIM] / mixed[:, HEAD_DIM:]
                for member in range(GROUP):
                    rows = slice(member * TILE, (member + 1) * TILE)
                    head = group * GROUP + member
                    spot = (pl.ds(base, TILE), slice(head * HEAD_DIM, (head + 1) * HEAD_DIM))
                    kept = attended[spot].astype(jnp.float32)
                    attended[spot] = jnp.where(inside[rows], answer[rows], kept).astype(jnp.bfloat16)
            return carry

        lax.fori_loop(start // TILE, (end + TILE - 1) // TILE, attend, 0)

    last_load.wait()
    projected = jnp.dot(attended[...], w_out[...], preferred_element_type=jnp.float32)
    residual = (tokens_ref[...].astype(jnp.float32) + projected).astype(jnp.bfloat16)
    residual_ref[...] = residual
    wide = residual.astype(jnp.float32)
    scale = lax.rsqrt(jnp.mean(wide * wide, axis=1, keepdims=True) + epsilon)
    normed_ref[...] = (wide * scale * ffn_gain_ref[...].reshape(1, -1)).astype(jnp.bfloat16)


def front(
    tokens,
    attn_gain,
    ffn_gain,
    w_query,
    w_key,
    w_value,
    w_out,
    key_cache,
    value_cache,
    lengths,
    cached,
    pick,
    ids,
    gates,
    replica_owner,
):
    count, width = tokens.shape
    any_space = pl.BlockSpec(memory_space=pl.ANY)
    vmem = pl.BlockSpec(memory_space=pltpu.VMEM)
    smem = pl.BlockSpec(memory_space=pltpu.SMEM)
    dma = pltpu.SemaphoreType.DMA
    bf16 = jnp.bfloat16
    rates = np.float32(rope_base) ** (-(np.arange(HEAD_DIM // 2, dtype=np.float32) * 2.0 / HEAD_DIM))
    inverse = jnp.asarray(np.concatenate([rates, rates])[None, :].astype(np.float32))
    return pl.pallas_call(
        front_kernel,
        out_shape=(
            jax.ShapeDtypeStruct((count, width), bf16),
            jax.ShapeDtypeStruct((count, width), bf16),
            jax.ShapeDtypeStruct((8, count), jnp.float32),
            jax.ShapeDtypeStruct((8, 128), jnp.int32),
        ),
        in_specs=[smem] * 3 + [vmem] * 7 + [any_space] * 6,
        out_specs=(vmem,) * 4,
        scratch_shapes=[
            pltpu.VMEM(w_query.shape, bf16),
            pltpu.VMEM(w_key.shape, bf16),
            pltpu.VMEM(w_value.shape, bf16),
            pltpu.VMEM(w_out.shape, bf16),
            pltpu.VMEM((3, KV_HEADS, CACHE, HEAD_DIM), bf16),
            pltpu.VMEM((3, KV_HEADS, CACHE, 2 * HEAD_DIM), bf16),
            pltpu.VMEM((KV_HEADS, count, HEAD_DIM), bf16),
            pltpu.VMEM((KV_HEADS, count, 2 * HEAD_DIM), bf16),
            pltpu.VMEM((HEADS, count, HEAD_DIM), bf16),
            pltpu.VMEM((count, HEADS * HEAD_DIM), bf16),
            dma((4,)),
            dma((3, KV_HEADS)),
            dma((3, KV_HEADS)),
        ],
        name="front",
        compiler_params=pltpu.CompilerParams(vmem_limit_bytes=58 << 20),
        cost_estimate=pl.CostEstimate(flops=12 * 10**9, bytes_accessed=60 * 10**6, transcendentals=10**7),
    )(
        lengths,
        cached,
        pick,
        tokens,
        attn_gain,
        ffn_gain,
        inverse,
        ids.T,
        gates.T,
        replica_owner.T,
        w_query,
        w_key,
        w_value,
        w_out,
        key_cache,
        value_cache,
    )


MESH = pl.DeviceIdType.MESH
SIDE = 4
SLOTS = 32
HALF = 128
WIDTH = 1536
HIDDEN = 768
CHUNK = 2 * SIDE * SLOTS
PARTNERS = [
    (dz, dx, dy, dc)
    for dz in range(SIDE)
    for dx in range(SIDE)
    for dy in range(SIDE)
    for dc in range(2)
    if (dz == 0) + (dx == 0) + (dy == 0) >= 2 and (dz, dx, dy, dc) != (0, 0, 0, 0)
]


def place():
    row, column = lax.axis_index("dp"), lax.axis_index("expert")
    return row // SIDE, row % SIDE, column // 2, column % 2


def device_at(dz, dx, dy, dc):
    z, x, y, c = place()
    row = ((z + dz) % SIDE) * SIDE + (x + dx) % SIDE
    return (row, ((y + dy) % SIDE) * 2 + (c + dc) % 2)


def along(half, offset, dc=0):
    return device_at(half * offset, (1 - half) * offset, 0, dc)


def across(half, offset):
    return device_at((1 - half) * offset, half * offset, 0, 0)


def send(source, landing, sem_s, sem_r, device):
    return pltpu.make_async_remote_copy(
        src_ref=source,
        dst_ref=landing,
        send_sem=sem_s,
        recv_sem=sem_r,
        device_id=device,
        device_id_type=MESH,
    )


def moe_kernel(
    rows_ref,
    table_ref,
    counts_ref,
    residual_ref,
    gate_up_ref,
    down_ref,
    out_ref,
    owner_ref,
    held,
    tables,
    packed,
    landed,
    done,
    back_rows,
    partial,
    given,
    total,
    gate_up,
    down,
    tallies,
    told,
    s_first,
    r_first,
    s_table,
    r_table,
    s_out,
    r_out,
    s_back,
    r_back,
    s_give,
    r_give,
    s_tally,
    r_tally,
    s_weight,
    r_weight,
    s_pass,
    r_pass,
    d_down,
    s_relay,
    r_relay,
    lent,
    s_lend,
    r_lend,
):
    z, x, y, c = place()
    barrier = pltpu.get_barrier_semaphore()
    for offsets in PARTNERS:
        pl.semaphore_signal(barrier, inc=1, device_id=device_at(*offsets), device_id_type=MESH)
    pl.semaphore_wait(barrier, len(PARTNERS))

    first = []
    for back in (1, 3, 2):
        for half in range(2):
            there = across(half, back)
            first.append(
                send(table_ref, tables.at[half, back], s_table.at[half, back], r_table.at[half, back], there)
            )
            if back != 2:
                first.append(
                    send(
                        rows_ref.at[pl.ds(half * HALF, HALF)],
                        held.at[half, back],
                        s_first.at[half, back],
                        r_first.at[half, back],
                        there,
                    )
                )
    for copy in first:
        copy.start()

    column = y * 2 + c
    shards = {}
    for dc in range(2):
        expert = (c + dc) % 2
        for dy in (1, 3, 0):
            source, landing = gate_up_ref.at[expert], gate_up.at[:, column]
            if dy == 0 and dc == 0:
                own_shard = pltpu.make_async_copy(source, landing, r_weight.at[dy, dc])
                own_shard.start()
            else:
                shards[dy, dc] = send(
                    source, landing, s_weight.at[dy, dc], r_weight.at[dy, dc], device_at(0, 0, dy, dc)
                )
                shards[dy, dc].start()
    own_down = pltpu.make_async_copy(down_ref.at[c], down, d_down)
    own_down.start()

    tallies[0] = counts_ref[...]
    legs = [
        [(0, 1, 0, 0), (0, 2, 0, 0), (0, 3, 0, 0)],
        [(1, 0, 0, 0), (2, 0, 0, 0), (3, 0, 0, 0)],
        [(0, 0, 1, 0), (0, 0, 2, 0), (0, 0, 3, 0)],
        [(0, 0, 0, 1)],
    ]

    def tally(leg):
        copies = [
            send(tallies.at[leg], told.at[leg, k], s_tally.at[leg, k], r_tally.at[leg, k], device_at(*offsets))
            for k, offsets in enumerate(legs[leg])
        ]
        for copy in copies:
            copy.start()
        return copies

    def add_tallies(leg, copies):
        held_so_far = tallies[leg]
        for k, copy in enumerate(copies):
            copy.wait()
            held_so_far = held_so_far + told[leg, k]
        return held_so_far

    telling = tally(0)

    held[0, 0] = rows_ref[0:HALF, :]
    held[1, 0] = rows_ref[HALF : 2 * HALF, :]
    tables[0, 0] = table_ref[...]
    tables[1, 0] = table_ref[...]
    line = lax.broadcasted_iota(jnp.int32, (CHUNK, HALF), 0)

    def copies_out(half, back):
        at = (1 - half) * x + half * z
        copies = []
        for dc in (1, 0):
            for offset in (2, 1, 3, 0):
                piece = packed.at[half, back, (at + offset) % SIDE, (c + dc) % 2]
                landing = landed.at[half, back, offset, dc]
                arrival = r_out.at[half, back, offset, dc]
                if offset == 0 and dc == 0:
                    copies.append(pltpu.make_async_copy(piece, landing, arrival))
                else:
                    copies.append(
                        send(piece, landing, s_out.at[half, back, offset, dc], arrival, along(half, offset, dc))
                    )
        return copies

    def pack(half, back):
        if half == 0:
            wanted = line + z * CHUNK
        else:
            wanted = (line // 64) * CHUNK + x * 64 + line % 64
        table = tables[half, back]
        hot = jnp.zeros((CHUNK, HALF), jnp.bool_)
        for k in range(4):
            code = table[k : k + 1, half * HALF : (half + 1) * HALF].astype(jnp.int32)
            hot = hot | (code == wanted)
        spread = jnp.dot(
            hot.astype(jnp.float32).astype(jnp.bfloat16),
            held[half, back],
            preferred_element_type=jnp.float32,
        ).astype(jnp.bfloat16)
        packed[half, back] = spread.reshape(SIDE, 2, SLOTS, WIDTH)
        for copy in copies_out(half, back):
            copy.start()

    def relay(half, side):
        rows = pl.ds(side * (HALF // 2), HALF // 2)
        return send(
            held.at[half, 1 + 2 * side, rows],
            held.at[half, 2, rows],
            s_relay.at[half, side],
            r_relay.at[half, side],
            across(half, 1 + 2 * side),
        )

    def arrive(half, back):
        send(
            table_ref,
            tables.at[half, back],
            s_table.at[half, back],
            r_table.at[half, back],
            across(half, back),
        ).wait_recv()
        if back == 2:
            for side in range(2):
                relay(half, side).wait_recv()
        else:
            send(
                rows_ref.at[pl.ds(half * HALF, HALF)],
                held.at[half, back],
                s_first.at[half, back],
                r_first.at[half, back],
                across(half, back),
            ).wait_recv()
            relay(half, back // 2).start()

    for half in range(2):
        pack(half, 0)
    for back in (1, 3, 2):
        for half in range(2):
            arrive(half, back)
        for half in range(2):
            pack(half, back)

    passing = []
    for dc in range(2):
        for side, (dy, onward, low) in enumerate(((1, 1, 0), (3, 3, 1))):
            owner = ((y + SIDE - dy) % SIDE) * 2 + (c + dc) % 2
            whole = gate_up.at[:, owner]
            piece = gate_up.at[:, owner, pl.ds(low * 48, 48)]
            send(whole, whole, s_weight.at[dy, dc], r_weight.at[dy, dc], device_at(0, 0, dy, dc)).wait_recv()
            copy = send(
                piece, piece, s_pass.at[side, dc], r_pass.at[side, dc], device_at(0, 0, onward, 0)
            )
            copy.start()
            passing.append(copy)

    tallies[1] = add_tallies(0, telling)
    telling = tally(1)

    own_down.wait()
    own_shard.wait()
    shards[0, 1].wait_recv()
    for copy in passing:
        copy.wait()

    def copies_back(half, back, own=True):
        copies = []
        for dc in (1, 0):
            for offset in (2, 1, 3, 0):
                if offset == 0 and dc == 0 and not own:
                    continue
                piece = done.at[half, back, offset, dc]
                landing = back_rows.at[half, back, offset, dc]
                arrival = r_back.at[half, back, offset, dc]
                if offset == 0 and dc == 0:
                    copies.append((pltpu.make_async_copy(piece, landing, arrival), False))
                else:
                    copies.append(
                        (
                            send(
                                piece,
                                landing,
                                s_back.at[half, back, offset, dc],
                                arrival,
                                along(half, SIDE - offset, dc),
                            ),
                            True,
                        )
                    )
        return copies

    last = (((1,), (1,)), ((), ()))

    def serve(step, carry):
        turn_at = step // 2
        half, back = step % 2, 2 - turn_at + 3 * (turn_at // 2) - 2 * (turn_at // 3)
        for copy in copies_out(half, back):
            copy.wait()
        arrived = landed[half, back].reshape(CHUNK, WIDTH)
        gate = lax.dot_general(
            arrived, gate_up[0].reshape(HIDDEN, WIDTH), last, preferred_element_type=jnp.float32
        )
        up = lax.dot_general(
            arrived, gate_up[1].reshape(HIDDEN, WIDTH), last, preferred_element_type=jnp.float32
        )
        hidden = (jnp.maximum(gate, 0.0) * up).astype(jnp.bfloat16)
        answer = lax.dot_general(
            hidden, down[...], last, preferred_element_type=jnp.float32
        )
        done[half, back] = answer.astype(jnp.bfloat16).reshape(SIDE, 2, SLOTS, WIDTH)
        for copy, _ in copies_back(half, back):
            copy.start()
        return carry

    lax.fori_loop(0, 2 * SIDE, serve, 0)
    tallies[2] = add_tallies(1, telling)
    telling = tally(2)

    turn, swap, slot = line // 64, (line // 32) % 2, line % 32

    def mix(half, back):
        for copy, remote in copies_back(half, back):
            if remote:
                copy.wait_recv()
            else:
                copy.wait()
        if half == 0:
            owner = z * SIDE + (x + turn) % SIDE
        else:
            owner = ((z + turn) % SIDE) * SIDE + x
        wanted = owner * 64 + ((c + swap) % 2) * 32 + slot
        table = tables[half, back]
        weight = jnp.zeros((CHUNK, HALF), jnp.float32)
        for k in range(4):
            code = table[k : k + 1, half * HALF : (half + 1) * HALF].astype(jnp.int32)
            gate = table[4 + k : 5 + k, half * HALF : (half + 1) * HALF]
            weight = weight + jnp.where(code == wanted, gate, 0.0)
        coarse = weight.astype(jnp.bfloat16)
        fine = (weight - coarse.astype(jnp.float32)).astype(jnp.bfloat16)
        came = back_rows[half, back].reshape(CHUNK, WIDTH)
        rows = (((0,), (0,)), ((), ()))
        return lax.dot_general(
            coarse, came, rows, preferred_element_type=jnp.float32
        ) + lax.dot_general(fine, came, rows, preferred_element_type=jnp.float32)

    def gift(half, back):
        return send(
            partial.at[half, back],
            given.at[half, back],
            s_give.at[half, back],
            r_give.at[half, back],
            across(half, SIDE - back),
        )

    def lend(half, side):
        rows = pl.ds(side * (HALF // 2), HALF // 2)
        return send(
            partial.at[half, 2, rows],
            lent.at[half, side],
            s_lend.at[half, side],
            r_lend.at[half, side],
            across(half, 3 - 2 * side),
        )

    for half in range(2):
        partial[half, 2] = mix(half, 2).astype(jnp.bfloat16)
        for side in range(2):
            lend(half, side).start()
    for side in range(2):
        back = 1 + 2 * side
        for half in range(2):
            share = mix(half, back)
            lend(half, side).wait_recv()
            rows = slice(side * (HALF // 2), (side + 1) * (HALF // 2))
            others = slice((1 - side) * (HALF // 2), (2 - side) * (HALF // 2))
            partial[half, back, rows] = (share[rows] + lent[half, side].astype(jnp.float32)).astype(jnp.bfloat16)
            partial[half, back, others] = share[others].astype(jnp.bfloat16)
            gift(half, back).start()
    tallies[3] = add_tallies(2, telling)
    telling = tally(3)
    for half in range(2):
        total[half] = mix(half, 0)
    tallied = add_tallies(3, telling)
    me = lax.axis_index("dp") * 8 + lax.axis_index("expert")
    lane = lax.broadcasted_iota(jnp.int32, tallied.shape, 1)
    mine = jnp.sum(jnp.where(lane == me, tallied, 0).astype(jnp.float32), axis=1, keepdims=True)
    owner_ref[...] = jnp.broadcast_to(mine, tallied.shape).astype(jnp.int32)
    for half in range(2):
        mixed = total[half]
        for back in (1, 3):
            gift(half, back).wait_recv()
            mixed = mixed + given[half, back].astype(jnp.float32)
        here = pl.ds(half * HALF, HALF)
        out_ref[here, :] = (residual_ref[here, :].astype(jnp.float32) + mixed).astype(jnp.bfloat16)

    for copy in first:
        copy.wait_send()
    for half in range(2):
        for side in range(2):
            relay(half, side).wait_send()
    for copy in shards.values():
        copy.wait_send()

    def settle(step, carry):
        half, back = step % 2, step // 2
        for copy, _ in copies_back(half, back, own=False):
            copy.wait_send()
        return carry

    lax.fori_loop(0, 2 * SIDE, settle, 0)
    for half in range(2):
        for back in (1, 3):
            gift(half, back).wait_send()
        for side in range(2):
            lend(half, side).wait_send()


def moe(rows, table, counts, residual, gate_up, down):
    any_space = pl.BlockSpec(memory_space=pl.ANY)
    vmem = pl.BlockSpec(memory_space=pltpu.VMEM)
    dma = pltpu.SemaphoreType.DMA
    chunks = (2, SIDE, SIDE, 2, SLOTS, WIDTH)
    halves = (2, SIDE, HALF, WIDTH)
    bf16 = jnp.bfloat16
    return pl.pallas_call(
        moe_kernel,
        out_shape=(
            jax.ShapeDtypeStruct((2 * HALF, WIDTH), bf16),
            jax.ShapeDtypeStruct((8, 128), jnp.int32),
        ),
        in_specs=[vmem, vmem, vmem, vmem, any_space, any_space],
        out_specs=(vmem, vmem),
        scratch_shapes=[
            pltpu.VMEM(halves, bf16),
            pltpu.VMEM((2, SIDE, 8, 2 * HALF), jnp.float32),
            pltpu.VMEM(chunks, bf16),
            pltpu.VMEM(chunks, bf16),
            pltpu.VMEM(chunks, bf16),
            pltpu.VMEM(chunks, bf16),
            pltpu.VMEM(halves, bf16),
            pltpu.VMEM(halves, bf16),
            pltpu.VMEM((2, HALF, WIDTH), jnp.float32),
            pltpu.VMEM((2, 8, 96, WIDTH), bf16),
            pltpu.VMEM((WIDTH, HIDDEN), bf16),
            pltpu.VMEM((4, 8, 128), jnp.int32),
            pltpu.VMEM((4, 3, 8, 128), jnp.int32),
            dma((2, SIDE)),
            dma((2, SIDE)),
            dma((2, SIDE)),
            dma((2, SIDE)),
            dma((2, SIDE, SIDE, 2)),
            dma((2, SIDE, SIDE, 2)),
            dma((2, SIDE, SIDE, 2)),
            dma((2, SIDE, SIDE, 2)),
            dma((2, SIDE)),
            dma((2, SIDE)),
            dma((4, 3)),
            dma((4, 3)),
            dma((SIDE, 2)),
            dma((SIDE, 2)),
            dma((2, 2)),
            dma((2, 2)),
            dma(()),
            dma((2, 2)),
            dma((2, 2)),
            pltpu.VMEM((2, 2, HALF // 2, WIDTH), bf16),
            dma((2, 2)),
            dma((2, 2)),
        ],
        name="moe",
        compiler_params=pltpu.CompilerParams(
            collective_id=1, has_side_effects=True, vmem_limit_bytes=60 << 20
        ),
        cost_estimate=pl.CostEstimate(flops=17 * 10**9, bytes_accessed=10**7, transcendentals=0),
    )(rows, table, counts, residual, gate_up, down)


def on_device(
    tokens,
    attn_gain,
    ffn_gain,
    w_query,
    w_key,
    w_value,
    w_out,
    key_cache,
    value_cache,
    req_lengths,
    cache_lengths,
    expert_ids,
    route_gate,
    replica_owner,
    replica_pick,
    w_gate_up,
    w_down,
):
    down = lax.all_gather(w_down, "expert", axis=1, tiled=True)
    residual, normed_mid, table, counts = front(
        tokens,
        attn_gain,
        ffn_gain,
        w_query,
        w_key,
        w_value,
        w_out,
        key_cache,
        value_cache,
        req_lengths,
        cache_lengths,
        replica_pick,
        expert_ids,
        route_gate,
        replica_owner,
    )
    layer_out, owner_counts = moe(
        normed_mid, table, counts, residual, w_gate_up.transpose(0, 2, 1, 3), down
    )
    return (layer_out, owner_counts[: w_gate_up.shape[0], 0][None, :])


def solution(mesh):
    in_specs = (
        P(("dp", "expert"), None),
        P(),
        P(),
        P(),
        P(),
        P(),
        P(),
        P(("dp", "expert"), None, None),
        P(("dp", "expert"), None, None),
        P(("dp", "expert"), None),
        P(("dp", "expert"), None),
        P(("dp", "expert"), None),
        P(("dp", "expert"), None),
        P(),
        P(("dp", "expert"), None),
        P("dp", "expert", None, None),
        P("dp", "expert", None),
    )
    out_specs = (P(("dp", "expert"), None), P(("dp", "expert"), None))
    return jax.shard_map(
        on_device, mesh=mesh, in_specs=in_specs, out_specs=out_specs, check_vma=False
    )
```

```python
import jax
import jax.numpy as jnp
import numpy as np
from jax import lax
from jax.experimental import pallas as pl
from jax.experimental.pallas import tpu as pltpu
from jax.sharding import PartitionSpec as P

HEADS = 12
KV_HEADS = 2
HEAD_DIM = 128


epsilon = 1e-06
rope_base = 1000000.0


GROUP = HEADS // KV_HEADS
TILE = 64
CACHE = 2048
OPEN = 1024


def front_kernel(
    lengths_ref,
    cached_ref,
    pick_ref,
    tokens_ref,
    attn_gain_ref,
    ffn_gain_ref,
    inverse_ref,
    ids_ref,
    gate_ref,
    owners_ref,
    w_query_hbm,
    w_key_hbm,
    w_value_hbm,
    w_out_hbm,
    keys_hbm,
    values_hbm,
    residual_ref,
    normed_ref,
    table_ref,
    counts_ref,
    w_query,
    w_key,
    w_value,
    w_out,
    keys,
    values,
    new_keys,
    new_values,
    queries,
    attended,
    sem_w,
    sem_k,
    sem_v,
):
    count = tokens_ref.shape[0]
    loads = [
        pltpu.make_async_copy(w_query_hbm, w_query, sem_w.at[0]),
        pltpu.make_async_copy(w_key_hbm, w_key, sem_w.at[1]),
        pltpu.make_async_copy(w_value_hbm, w_value, sem_w.at[2]),
    ]

    def cache_loads(request):
        copies = []
        for group in range(KV_HEADS):
            lanes = pl.ds(group * HEAD_DIM, HEAD_DIM)
            copies.append(
                pltpu.make_async_copy(
                    keys_hbm.at[request, :, lanes], keys.at[request, group], sem_k.at[request, group]
                )
            )
            copies.append(
                pltpu.make_async_copy(
                    values_hbm.at[request, :, lanes],
                    values.at[request, group, :, pl.ds(0, HEAD_DIM)],
                    sem_v.at[request, group],
                )
            )
        return copies

    last_load = pltpu.make_async_copy(w_out_hbm, w_out, sem_w.at[3])
    for copy in loads:
        copy.start()
    for request in range(3):
        for copy in cache_loads(request):
            copy.start()
    last_load.start()

    starts = [0, lengths_ref[0, 0], lengths_ref[0, 0] + lengths_ref[0, 1]]
    ends = [starts[1], starts[2], count]
    cached = [cached_ref[0, request] for request in range(3)]

    def by_request(token, values_of):
        return jnp.where(
            token < starts[1], values_of[0], jnp.where(token < starts[2], values_of[1], values_of[2])
        )

    lane = lax.broadcasted_iota(jnp.int32, (count, 128), 1)
    row = lax.broadcasted_iota(jnp.int32, (count, 128), 0)
    expert = lax.broadcasted_iota(jnp.int32, (32, count), 0)
    ids = [ids_ref[k : k + 1, :] for k in range(4)]
    hots = [(ids[k] == expert).astype(jnp.float32) for k in range(4)]
    hot = (hots[0] + hots[1] + hots[2] + hots[3]).astype(jnp.bfloat16)
    sooner = lax.broadcasted_iota(jnp.int32, (count, count), 0)
    later = lax.broadcasted_iota(jnp.int32, (count, count), 1)
    before = jnp.dot(
        hot,
        ((later // 32 == sooner // 32) & (sooner < later)).astype(jnp.float32).astype(jnp.bfloat16),
        preferred_element_type=jnp.float32,
    )
    line = lax.broadcasted_iota(jnp.int32, (8, count), 0)
    offset = lax.broadcasted_iota(jnp.int32, (1, count), 1) // 32 % 4 * 8
    table = jnp.zeros((8, count), jnp.float32)
    for k in range(4):
        rank = jnp.sum(hots[k] * before, axis=0, keepdims=True)
        code = (ids[k] * 32 + offset).astype(jnp.float32) + rank
        table = jnp.where(line == k, code, table)
        table = jnp.where(line == 4 + k, gate_ref[k : k + 1, :], table)
    table_ref[...] = table

    members = lax.broadcasted_iota(jnp.int32, (8, count), 1)
    last = (((1,), (1,)), ((), ()))
    per_block = lax.dot_general(
        (members // 32 == line).astype(jnp.float32).astype(jnp.bfloat16),
        hot,
        last,
        preferred_element_type=jnp.float32,
    )
    place_of = lax.broadcasted_iota(jnp.int32, (8, 32), 0)
    per_owner = jnp.zeros((8, 32), jnp.float32)
    for block in range(8):
        owner = owners_ref[pl.ds(pick_ref[0, block], 1), :]
        per_owner = per_owner + jnp.where(place_of == owner, per_block[block : block + 1, :], 0.0)
    expert_row = lax.broadcasted_iota(jnp.int32, (32, 128), 0)
    owner_lane = lax.broadcasted_iota(jnp.int32, (32, 128), 1)
    own_line = lax.broadcasted_iota(jnp.int32, (8, 128), 0)
    own_lane = lax.broadcasted_iota(jnp.int32, (8, 128), 1)
    tallied = jnp.zeros((8, 128), jnp.float32)
    for j in range(2):
        moved = jnp.dot(
            per_owner.astype(jnp.bfloat16),
            (expert_row == owner_lane // 8 * 2 + j).astype(jnp.float32).astype(jnp.bfloat16),
            preferred_element_type=jnp.float32,
        )
        own = jnp.sum(jnp.where(own_lane % 8 == own_line, moved, 0.0), axis=0, keepdims=True)
        tallied = jnp.where(own_line == j, own, tallied)
    counts_ref[...] = tallied.astype(jnp.int32)

    for request in range(3):
        for group in range(KV_HEADS):
            values[request, group, :, HEAD_DIM:] = jnp.ones((CACHE, HEAD_DIM), jnp.bfloat16)
    for group in range(KV_HEADS):
        new_values[group, :, HEAD_DIM:] = jnp.ones((count, HEAD_DIM), jnp.bfloat16)

    wide = tokens_ref[...].astype(jnp.float32)
    scale = lax.rsqrt(jnp.mean(wide * wide, axis=1, keepdims=True) + epsilon)
    normed = (wide * scale * attn_gain_ref[...].reshape(1, -1)).astype(jnp.bfloat16)

    position = row + by_request(row, [cached[0], cached[1] - starts[1], cached[2] - starts[2]])
    angle = position.astype(jnp.float32) * inverse_ref[...]
    cosine = jnp.cos(angle)
    sine = jnp.sin(angle)
    sine = jnp.where(lane < HEAD_DIM // 2, -sine, sine)

    def turned(head):
        return (head * cosine + pltpu.roll(head, HEAD_DIM // 2, 1) * sine).astype(jnp.bfloat16)

    loads[0].wait()
    for part in range(HEADS // 2):
        pair = jnp.dot(
            normed,
            w_query[:, part * 256 : (part + 1) * 256],
            preferred_element_type=jnp.float32,
        )
        for side in range(2):
            queries[part * 2 + side] = turned(pair[:, side * HEAD_DIM : (side + 1) * HEAD_DIM])
    loads[1].wait()
    fresh_keys = jnp.dot(normed, w_key[...], preferred_element_type=jnp.float32)
    loads[2].wait()
    fresh_values = jnp.dot(normed, w_value[...], preferred_element_type=jnp.float32)
    for group in range(KV_HEADS):
        lanes = slice(group * HEAD_DIM, (group + 1) * HEAD_DIM)
        new_keys[group] = turned(fresh_keys[:, lanes])
        new_values[group, :, 0:HEAD_DIM] = fresh_values[:, lanes].astype(jnp.bfloat16)

    factor = HEAD_DIM ** (-0.5) * 1.4426950408889634
    stack = GROUP * TILE
    lowest = -jnp.inf
    for request in range(3):
        for copy in cache_loads(request):
            copy.wait()
        start, end, filled = starts[request], ends[request], cached[request]

        def attend(tile, carry, request=request, start=start, end=end, filled=filled):
            base = pl.multiple_of(tile * TILE, TILE)
            token = base + lax.broadcasted_iota(jnp.int32, (stack, 128), 0) % TILE
            here = filled + token - start
            slot = lax.broadcasted_iota(jnp.int32, (stack, 128), 1)
            near = (slot == 0) | (here - slot < CACHE)
            open_slot = OPEN + lax.broadcasted_iota(jnp.int32, (1, CACHE - OPEN), 1)
            bias = jnp.where(open_slot < filled, 0.0, lowest)
            fresh = lax.broadcasted_iota(jnp.int32, (stack, count), 1)
            asking = base + lax.broadcasted_iota(jnp.int32, (stack, count), 0) % TILE
            seen = (fresh >= start) & (fresh <= asking)
            inside = (token >= start) & (token < end)
            for group in range(KV_HEADS):
                asked = queries[group * GROUP : (group + 1) * GROUP, pl.ds(base, TILE), :].reshape(
                    stack, HEAD_DIM
                )

                def score(block):
                    return lax.dot_general(asked, block, last, preferred_element_type=jnp.float32)

                parts = [
                    jnp.where(near, score(keys[request, group, 0:128, :]), lowest),
                    score(keys[request, group, 128:OPEN, :]),
                    score(keys[request, group, OPEN:CACHE, :]) + bias,
                    jnp.where(seen, score(new_keys[group]), lowest),
                ]
                peak = jnp.max(parts[0], axis=1, keepdims=True)
                for part in parts[1:]:
                    peak = jnp.maximum(peak, jnp.max(part, axis=1, keepdims=True))
                peak = peak * factor
                blocks = [
                    values[request, group, 0:128, :],
                    values[request, group, 128:OPEN, :],
                    values[request, group, OPEN:CACHE, :],
                    new_values[group],
                ]
                mixed = jnp.zeros((stack, 2 * HEAD_DIM), jnp.float32)
                for part, block in zip(parts, blocks):
                    weight = jnp.exp2(part * factor - peak).astype(jnp.bfloat16)
                    mixed = mixed + jnp.dot(weight, block, preferred_element_type=jnp.float32)
                answer = mixed[:, 0:HEAD_DIM] / mixed[:, HEAD_DIM:]
                for member in range(GROUP):
                    rows = slice(member * TILE, (member + 1) * TILE)
                    head = group * GROUP + member
                    spot = (pl.ds(base, TILE), slice(head * HEAD_DIM, (head + 1) * HEAD_DIM))
                    kept = attended[spot].astype(jnp.float32)
                    attended[spot] = jnp.where(inside[rows], answer[rows], kept).astype(jnp.bfloat16)
            return carry

        lax.fori_loop(start // TILE, (end + TILE - 1) // TILE, attend, 0)

    last_load.wait()
    projected = jnp.dot(attended[...], w_out[...], preferred_element_type=jnp.float32)
    residual = (tokens_ref[...].astype(jnp.float32) + projected).astype(jnp.bfloat16)
    residual_ref[...] = residual
    wide = residual.astype(jnp.float32)
    scale = lax.rsqrt(jnp.mean(wide * wide, axis=1, keepdims=True) + epsilon)
    normed_ref[...] = (wide * scale * ffn_gain_ref[...].reshape(1, -1)).astype(jnp.bfloat16)


def front(
    tokens,
    attn_gain,
    ffn_gain,
    w_query,
    w_key,
    w_value,
    w_out,
    key_cache,
    value_cache,
    lengths,
    cached,
    pick,
    ids,
    gates,
    replica_owner,
):
    count, width = tokens.shape
    any_space = pl.BlockSpec(memory_space=pl.ANY)
    vmem = pl.BlockSpec(memory_space=pltpu.VMEM)
    smem = pl.BlockSpec(memory_space=pltpu.SMEM)
    dma = pltpu.SemaphoreType.DMA
    bf16 = jnp.bfloat16
    rates = np.float32(rope_base) ** (-(np.arange(HEAD_DIM // 2, dtype=np.float32) * 2.0 / HEAD_DIM))
    inverse = jnp.asarray(np.concatenate([rates, rates])[None, :].astype(np.float32))
    return pl.pallas_call(
        front_kernel,
        out_shape=(
            jax.ShapeDtypeStruct((count, width), bf16),
            jax.ShapeDtypeStruct((count, width), bf16),
            jax.ShapeDtypeStruct((8, count), jnp.float32),
            jax.ShapeDtypeStruct((8, 128), jnp.int32),
        ),
        in_specs=[smem] * 3 + [vmem] * 7 + [any_space] * 6,
        out_specs=(vmem,) * 4,
        scratch_shapes=[
            pltpu.VMEM(w_query.shape, bf16),
            pltpu.VMEM(w_key.shape, bf16),
            pltpu.VMEM(w_value.shape, bf16),
            pltpu.VMEM(w_out.shape, bf16),
            pltpu.VMEM((3, KV_HEADS, CACHE, HEAD_DIM), bf16),
            pltpu.VMEM((3, KV_HEADS, CACHE, 2 * HEAD_DIM), bf16),
            pltpu.VMEM((KV_HEADS, count, HEAD_DIM), bf16),
            pltpu.VMEM((KV_HEADS, count, 2 * HEAD_DIM), bf16),
            pltpu.VMEM((HEADS, count, HEAD_DIM), bf16),
            pltpu.VMEM((count, HEADS * HEAD_DIM), bf16),
            dma((4,)),
            dma((3, KV_HEADS)),
            dma((3, KV_HEADS)),
        ],
        name="front",
        compiler_params=pltpu.CompilerParams(vmem_limit_bytes=58 << 20),
        cost_estimate=pl.CostEstimate(flops=12 * 10**9, bytes_accessed=60 * 10**6, transcendentals=10**7),
    )(
        lengths,
        cached,
        pick,
        tokens,
        attn_gain,
        ffn_gain,
        inverse,
        ids.T,
        gates.T,
        replica_owner.T,
        w_query,
        w_key,
        w_value,
        w_out,
        key_cache,
        value_cache,
    )


MESH = pl.DeviceIdType.MESH
SIDE = 4
SLOTS = 32
HALF = 128
WIDTH = 1536
HIDDEN = 768
CHUNK = 2 * SIDE * SLOTS
PARTNERS = [
    (dz, dx, dy, dc)
    for dz in range(SIDE)
    for dx in range(SIDE)
    for dy in range(SIDE)
    for dc in range(2)
    if (dz == 0) + (dx == 0) + (dy == 0) >= 2 and (dz, dx, dy, dc) != (0, 0, 0, 0)
]


def place():
    row, column = lax.axis_index("dp"), lax.axis_index("expert")
    return row // SIDE, row % SIDE, column // 2, column % 2


def device_at(dz, dx, dy, dc):
    z, x, y, c = place()
    row = ((z + dz) % SIDE) * SIDE + (x + dx) % SIDE
    return (row, ((y + dy) % SIDE) * 2 + (c + dc) % 2)


def along(half, offset, dc=0):
    return device_at(half * offset, (1 - half) * offset, 0, dc)


def across(half, offset):
    return device_at((1 - half) * offset, half * offset, 0, 0)


def send(source, landing, sem_s, sem_r, device):
    return pltpu.make_async_remote_copy(
        src_ref=source,
        dst_ref=landing,
        send_sem=sem_s,
        recv_sem=sem_r,
        device_id=device,
        device_id_type=MESH,
    )


def moe_kernel(
    rows_ref,
    table_ref,
    counts_ref,
    residual_ref,
    gate_up_ref,
    down_a,
    down_b,
    down_c,
    down_d,
    out_ref,
    owner_ref,
    held,
    tables,
    packed,
    landed,
    done,
    back_rows,
    partial,
    given,
    total,
    gate_up,
    down,
    tallies,
    told,
    s_first,
    r_first,
    s_table,
    r_table,
    s_out,
    r_out,
    s_back,
    r_back,
    s_give,
    r_give,
    s_tally,
    r_tally,
    s_weight,
    r_weight,
    s_pass,
    r_pass,
    d_down,
    s_down,
    r_down,
    s_relay,
    r_relay,
    lent,
    s_lend,
    r_lend,
):
    down_refs = (down_a, down_b, down_c, down_d)
    z, x, y, c = place()
    barrier = pltpu.get_barrier_semaphore()
    for offsets in PARTNERS:
        pl.semaphore_signal(barrier, inc=1, device_id=device_at(*offsets), device_id_type=MESH)
    pl.semaphore_wait(barrier, len(PARTNERS))

    first = []
    for back in (1, 3, 2):
        for half in range(2):
            there = across(half, back)
            first.append(
                send(table_ref, tables.at[half, back], s_table.at[half, back], r_table.at[half, back], there)
            )
            if back != 2:
                first.append(
                    send(
                        rows_ref.at[pl.ds(half * HALF, HALF)],
                        held.at[half, back],
                        s_first.at[half, back],
                        r_first.at[half, back],
                        there,
                    )
                )
    for copy in first:
        copy.start()

    column = y * 2 + c
    shards = {}
    for dc in range(2):
        expert = (c + dc) % 2
        for dy in (1, 3, 0):
            source, landing = gate_up_ref.at[expert], gate_up.at[:, column]
            if dy == 0 and dc == 0:
                own_shard = pltpu.make_async_copy(source, landing, r_weight.at[dy, dc])
                own_shard.start()
            else:
                shards[dy, dc] = send(
                    source, landing, s_weight.at[dy, dc], r_weight.at[dy, dc], device_at(0, 0, dy, dc)
                )
                shards[dy, dc].start()
    near_down, far_down = [], []
    for back, shard in enumerate(down_refs):
        spot = down.at[((y + SIDE - back) % SIDE) * 2 + c]
        near_down.append(pltpu.make_async_copy(shard.at[c], spot, d_down.at[back]))
        far_down.append(
            send(shard.at[1 - c], spot, s_down.at[back], r_down.at[back], device_at(0, 0, 0, 1))
        )
    for copy in near_down + far_down:
        copy.start()

    tallies[0] = counts_ref[...]
    legs = [
        [(0, 1, 0, 0), (0, 2, 0, 0), (0, 3, 0, 0)],
        [(1, 0, 0, 0), (2, 0, 0, 0), (3, 0, 0, 0)],
        [(0, 0, 1, 0), (0, 0, 2, 0), (0, 0, 3, 0)],
        [(0, 0, 0, 1)],
    ]

    def tally(leg):
        copies = [
            send(tallies.at[leg], told.at[leg, k], s_tally.at[leg, k], r_tally.at[leg, k], device_at(*offsets))
            for k, offsets in enumerate(legs[leg])
        ]
        for copy in copies:
            copy.start()
        return copies

    def add_tallies(leg, copies):
        held_so_far = tallies[leg]
        for k, copy in enumerate(copies):
            copy.wait()
            held_so_far = held_so_far + told[leg, k]
        return held_so_far

    telling = tally(0)

    held[0, 0] = rows_ref[0:HALF, :]
    held[1, 0] = rows_ref[HALF : 2 * HALF, :]
    tables[0, 0] = table_ref[...]
    tables[1, 0] = table_ref[...]
    line = lax.broadcasted_iota(jnp.int32, (CHUNK, HALF), 0)

    def copies_out(half, back):
        at = (1 - half) * x + half * z
        copies = []
        for dc in (1, 0):
            for offset in (2, 1, 3, 0):
                piece = packed.at[half, back, (at + offset) % SIDE, (c + dc) % 2]
                landing = landed.at[half, back, offset, dc]
                arrival = r_out.at[half, back, offset, dc]
                if offset == 0 and dc == 0:
                    copies.append(pltpu.make_async_copy(piece, landing, arrival))
                else:
                    copies.append(
                        send(piece, landing, s_out.at[half, back, offset, dc], arrival, along(half, offset, dc))
                    )
        return copies

    def pack(half, back):
        if half == 0:
            wanted = line + z * CHUNK
        else:
            wanted = (line // 64) * CHUNK + x * 64 + line % 64
        table = tables[half, back]
        hot = jnp.zeros((CHUNK, HALF), jnp.bool_)
        for k in range(4):
            code = table[k : k + 1, half * HALF : (half + 1) * HALF].astype(jnp.int32)
            hot = hot | (code == wanted)
        spread = jnp.dot(
            hot.astype(jnp.float32).astype(jnp.bfloat16),
            held[half, back],
            preferred_element_type=jnp.float32,
        ).astype(jnp.bfloat16)
        packed[half, back] = spread.reshape(SIDE, 2, SLOTS, WIDTH)
        for copy in copies_out(half, back):
            copy.start()

    def relay(half, side):
        rows = pl.ds(side * (HALF // 2), HALF // 2)
        return send(
            held.at[half, 1 + 2 * side, rows],
            held.at[half, 2, rows],
            s_relay.at[half, side],
            r_relay.at[half, side],
            across(half, 1 + 2 * side),
        )

    def arrive(half, back):
        send(
            table_ref,
            tables.at[half, back],
            s_table.at[half, back],
            r_table.at[half, back],
            across(half, back),
        ).wait_recv()
        if back == 2:
            for side in range(2):
                relay(half, side).wait_recv()
        else:
            send(
                rows_ref.at[pl.ds(half * HALF, HALF)],
                held.at[half, back],
                s_first.at[half, back],
                r_first.at[half, back],
                across(half, back),
            ).wait_recv()
            relay(half, back // 2).start()

    for half in range(2):
        pack(half, 0)
    for back in (1, 3, 2):
        for half in range(2):
            arrive(half, back)
        for half in range(2):
            pack(half, back)

    passing = []
    for dc in range(2):
        for side, (dy, onward, low) in enumerate(((1, 1, 0), (3, 3, 1))):
            owner = ((y + SIDE - dy) % SIDE) * 2 + (c + dc) % 2
            whole = gate_up.at[:, owner]
            piece = gate_up.at[:, owner, pl.ds(low * 48, 48)]
            send(whole, whole, s_weight.at[dy, dc], r_weight.at[dy, dc], device_at(0, 0, dy, dc)).wait_recv()
            copy = send(
                piece, piece, s_pass.at[side, dc], r_pass.at[side, dc], device_at(0, 0, onward, 0)
            )
            copy.start()
            passing.append(copy)

    tallies[1] = add_tallies(0, telling)
    telling = tally(1)

    for copy in near_down:
        copy.wait()
    for copy in far_down:
        copy.wait_recv()
    own_shard.wait()
    shards[0, 1].wait_recv()
    for copy in passing:
        copy.wait()

    def copies_back(half, back, own=True):
        copies = []
        for dc in (1, 0):
            for offset in (2, 1, 3, 0):
                if offset == 0 and dc == 0 and not own:
                    continue
                piece = done.at[half, back, offset, dc]
                landing = back_rows.at[half, back, offset, dc]
                arrival = r_back.at[half, back, offset, dc]
                if offset == 0 and dc == 0:
                    copies.append((pltpu.make_async_copy(piece, landing, arrival), False))
                else:
                    copies.append(
                        (
                            send(
                                piece,
                                landing,
                                s_back.at[half, back, offset, dc],
                                arrival,
                                along(half, SIDE - offset, dc),
                            ),
                            True,
                        )
                    )
        return copies

    last = (((1,), (1,)), ((), ()))

    def serve(step, carry):
        turn_at = step // 2
        half, back = step % 2, 2 - turn_at + 3 * (turn_at // 2) - 2 * (turn_at // 3)
        for copy in copies_out(half, back):
            copy.wait()
        arrived = landed[half, back].reshape(CHUNK, WIDTH)
        gate = lax.dot_general(
            arrived, gate_up[0].reshape(HIDDEN, WIDTH), last, preferred_element_type=jnp.float32
        )
        up = lax.dot_general(
            arrived, gate_up[1].reshape(HIDDEN, WIDTH), last, preferred_element_type=jnp.float32
        )
        hidden = (jnp.maximum(gate, 0.0) * up).astype(jnp.bfloat16)
        answer = lax.dot_general(
            hidden, down[...].reshape(WIDTH, HIDDEN), last, preferred_element_type=jnp.float32
        )
        done[half, back] = answer.astype(jnp.bfloat16).reshape(SIDE, 2, SLOTS, WIDTH)
        for copy, _ in copies_back(half, back):
            copy.start()
        return carry

    lax.fori_loop(0, 2 * SIDE, serve, 0)
    tallies[2] = add_tallies(1, telling)
    telling = tally(2)

    turn, swap, slot = line // 64, (line // 32) % 2, line % 32

    def mix(half, back):
        for copy, remote in copies_back(half, back):
            if remote:
                copy.wait_recv()
            else:
                copy.wait()
        if half == 0:
            owner = z * SIDE + (x + turn) % SIDE
        else:
            owner = ((z + turn) % SIDE) * SIDE + x
        wanted = owner * 64 + ((c + swap) % 2) * 32 + slot
        table = tables[half, back]
        weight = jnp.zeros((CHUNK, HALF), jnp.float32)
        for k in range(4):
            code = table[k : k + 1, half * HALF : (half + 1) * HALF].astype(jnp.int32)
            gate = table[4 + k : 5 + k, half * HALF : (half + 1) * HALF]
            weight = weight + jnp.where(code == wanted, gate, 0.0)
        coarse = weight.astype(jnp.bfloat16)
        fine = (weight - coarse.astype(jnp.float32)).astype(jnp.bfloat16)
        came = back_rows[half, back].reshape(CHUNK, WIDTH)
        rows = (((0,), (0,)), ((), ()))
        return lax.dot_general(
            coarse, came, rows, preferred_element_type=jnp.float32
        ) + lax.dot_general(fine, came, rows, preferred_element_type=jnp.float32)

    def gift(half, back):
        return send(
            partial.at[half, back],
            given.at[half, back],
            s_give.at[half, back],
            r_give.at[half, back],
            across(half, SIDE - back),
        )

    def lend(half, side):
        rows = pl.ds(side * (HALF // 2), HALF // 2)
        return send(
            partial.at[half, 2, rows],
            lent.at[half, side],
            s_lend.at[half, side],
            r_lend.at[half, side],
            across(half, 3 - 2 * side),
        )

    for half in range(2):
        partial[half, 2] = mix(half, 2).astype(jnp.bfloat16)
        for side in range(2):
            lend(half, side).start()
    for side in range(2):
        back = 1 + 2 * side
        for half in range(2):
            share = mix(half, back)
            lend(half, side).wait_recv()
            rows = slice(side * (HALF // 2), (side + 1) * (HALF // 2))
            others = slice((1 - side) * (HALF // 2), (2 - side) * (HALF // 2))
            partial[half, back, rows] = (share[rows] + lent[half, side].astype(jnp.float32)).astype(jnp.bfloat16)
            partial[half, back, others] = share[others].astype(jnp.bfloat16)
            gift(half, back).start()
    tallies[3] = add_tallies(2, telling)
    telling = tally(3)
    for half in range(2):
        total[half] = mix(half, 0)
    tallied = add_tallies(3, telling)
    me = lax.axis_index("dp") * 8 + lax.axis_index("expert")
    lane = lax.broadcasted_iota(jnp.int32, tallied.shape, 1)
    mine = jnp.sum(jnp.where(lane == me, tallied, 0).astype(jnp.float32), axis=1, keepdims=True)
    line_of = lax.broadcasted_iota(jnp.int32, tallied.shape, 0)
    owned = jnp.sum(jnp.where(line_of == lane, mine, 0.0), axis=0, keepdims=True)
    owner_ref[...] = owned[:, 0:2].astype(jnp.int32)
    for half in range(2):
        mixed = total[half]
        for back in (1, 3):
            gift(half, back).wait_recv()
            mixed = mixed + given[half, back].astype(jnp.float32)
        here = pl.ds(half * HALF, HALF)
        out_ref[here, :] = (residual_ref[here, :].astype(jnp.float32) + mixed).astype(jnp.bfloat16)

    for copy in first:
        copy.wait_send()
    for half in range(2):
        for side in range(2):
            relay(half, side).wait_send()
    for copy in list(shards.values()) + far_down:
        copy.wait_send()

    def settle(step, carry):
        half, back = step % 2, step // 2
        for copy, _ in copies_back(half, back, own=False):
            copy.wait_send()
        return carry

    lax.fori_loop(0, 2 * SIDE, settle, 0)
    for half in range(2):
        for back in (1, 3):
            gift(half, back).wait_send()
        for side in range(2):
            lend(half, side).wait_send()


def moe(rows, table, counts, residual, gate_up, downs):
    any_space = pl.BlockSpec(memory_space=pl.ANY)
    vmem = pl.BlockSpec(memory_space=pltpu.VMEM)
    dma = pltpu.SemaphoreType.DMA
    chunks = (2, SIDE, SIDE, 2, SLOTS, WIDTH)
    halves = (2, SIDE, HALF, WIDTH)
    bf16 = jnp.bfloat16
    return pl.pallas_call(
        moe_kernel,
        out_shape=(
            jax.ShapeDtypeStruct((2 * HALF, WIDTH), bf16),
            jax.ShapeDtypeStruct((1, 2), jnp.int32),
        ),
        in_specs=[vmem] * 4 + [any_space] * 5,
        out_specs=(vmem, vmem),
        scratch_shapes=[
            pltpu.VMEM(halves, bf16),
            pltpu.VMEM((2, SIDE, 8, 2 * HALF), jnp.float32),
            pltpu.VMEM(chunks, bf16),
            pltpu.VMEM(chunks, bf16),
            pltpu.VMEM(chunks, bf16),
            pltpu.VMEM(chunks, bf16),
            pltpu.VMEM(halves, bf16),
            pltpu.VMEM(halves, bf16),
            pltpu.VMEM((2, HALF, WIDTH), jnp.float32),
            pltpu.VMEM((2, 8, 96, WIDTH), bf16),
            pltpu.VMEM((8, 192, HIDDEN), bf16),
            pltpu.VMEM((4, 8, 128), jnp.int32),
            pltpu.VMEM((4, 3, 8, 128), jnp.int32),
            dma((2, SIDE)),
            dma((2, SIDE)),
            dma((2, SIDE)),
            dma((2, SIDE)),
            dma((2, SIDE, SIDE, 2)),
            dma((2, SIDE, SIDE, 2)),
            dma((2, SIDE, SIDE, 2)),
            dma((2, SIDE, SIDE, 2)),
            dma((2, SIDE)),
            dma((2, SIDE)),
            dma((4, 3)),
            dma((4, 3)),
            dma((SIDE, 2)),
            dma((SIDE, 2)),
            dma((2, 2)),
            dma((2, 2)),
            dma((SIDE,)),
            dma((SIDE,)),
            dma((SIDE,)),
            dma((2, 2)),
            dma((2, 2)),
            pltpu.VMEM((2, 2, HALF // 2, WIDTH), bf16),
            dma((2, 2)),
            dma((2, 2)),
        ],
        name="moe",
        compiler_params=pltpu.CompilerParams(
            collective_id=1, has_side_effects=True, vmem_limit_bytes=60 << 20
        ),
        cost_estimate=pl.CostEstimate(flops=17 * 10**9, bytes_accessed=10**7, transcendentals=0),
    )(rows, table, counts, residual, gate_up, *downs)


def on_device(
    tokens,
    attn_gain,
    ffn_gain,
    w_query,
    w_key,
    w_value,
    w_out,
    key_cache,
    value_cache,
    req_lengths,
    cache_lengths,
    expert_ids,
    route_gate,
    replica_owner,
    replica_pick,
    w_gate_up,
    w_down,
):
    columns = lax.axis_size("expert")
    downs = [w_down] + [
        lax.ppermute(w_down, "expert", [(i, (i + 2 * k) % columns) for i in range(columns)])
        for k in range(1, columns // 2)
    ]
    residual, normed_mid, table, counts = front(
        tokens,
        attn_gain,
        ffn_gain,
        w_query,
        w_key,
        w_value,
        w_out,
        key_cache,
        value_cache,
        req_lengths,
        cache_lengths,
        replica_pick,
        expert_ids,
        route_gate,
        replica_owner,
    )
    return moe(
        normed_mid, table, counts, residual, w_gate_up.transpose(0, 2, 1, 3), downs
    )


def solution(mesh):
    in_specs = (
        P(("dp", "expert"), None),
        P(),
        P(),
        P(),
        P(),
        P(),
        P(),
        P(("dp", "expert"), None, None),
        P(("dp", "expert"), None, None),
        P(("dp", "expert"), None),
        P(("dp", "expert"), None),
        P(("dp", "expert"), None),
        P(("dp", "expert"), None),
        P(),
        P(("dp", "expert"), None),
        P("dp", "expert", None, None),
        P("dp", "expert", None),
    )
    out_specs = (P(("dp", "expert"), None), P(("dp", "expert"), None))
    return jax.shard_map(
        on_device, mesh=mesh, in_specs=in_specs, out_specs=out_specs, check_vma=False
    )
```

```python
import jax
import jax.numpy as jnp
import numpy as np
from jax import lax
from jax.experimental import pallas as pl
from jax.experimental.pallas import tpu as pltpu
from jax.sharding import PartitionSpec as P

HEADS = 12
KV_HEADS = 2
HEAD_DIM = 128


epsilon = 1e-06
rope_base = 1000000.0


GROUP = HEADS // KV_HEADS
TILE = 64
CACHE = 2048
OPEN = 1024


def front_kernel(
    lengths_ref,
    cached_ref,
    pick_ref,
    tokens_ref,
    attn_gain_ref,
    ffn_gain_ref,
    inverse_ref,
    ids_ref,
    gate_ref,
    owners_ref,
    w_query_hbm,
    w_key_hbm,
    w_value_hbm,
    w_out_hbm,
    keys_hbm,
    values_hbm,
    residual_ref,
    normed_ref,
    table_ref,
    counts_ref,
    w_query,
    w_key,
    w_value,
    w_out,
    keys,
    values,
    new_keys,
    new_values,
    queries,
    attended,
    sem_w,
    sem_k,
    sem_v,
):
    count = tokens_ref.shape[0]
    loads = [
        pltpu.make_async_copy(w_query_hbm, w_query, sem_w.at[0]),
        pltpu.make_async_copy(w_key_hbm, w_key, sem_w.at[1]),
        pltpu.make_async_copy(w_value_hbm, w_value, sem_w.at[2]),
    ]

    def cache_loads(request):
        copies = []
        for group in range(KV_HEADS):
            lanes = pl.ds(group * HEAD_DIM, HEAD_DIM)
            copies.append(
                pltpu.make_async_copy(
                    keys_hbm.at[request, :, lanes], keys.at[request, group], sem_k.at[request, group]
                )
            )
            copies.append(
                pltpu.make_async_copy(
                    values_hbm.at[request, :, lanes],
                    values.at[request, group, :, pl.ds(0, HEAD_DIM)],
                    sem_v.at[request, group],
                )
            )
        return copies

    last_load = pltpu.make_async_copy(w_out_hbm, w_out, sem_w.at[3])
    for copy in loads:
        copy.start()
    for request in range(3):
        for copy in cache_loads(request):
            copy.start()
    last_load.start()

    starts = [0, lengths_ref[0, 0], lengths_ref[0, 0] + lengths_ref[0, 1]]
    ends = [starts[1], starts[2], count]
    cached = [cached_ref[0, request] for request in range(3)]

    def by_request(token, values_of):
        return jnp.where(
            token < starts[1], values_of[0], jnp.where(token < starts[2], values_of[1], values_of[2])
        )

    lane = lax.broadcasted_iota(jnp.int32, (count, 128), 1)
    row = lax.broadcasted_iota(jnp.int32, (count, 128), 0)
    expert = lax.broadcasted_iota(jnp.int32, (32, count), 0)
    ids = [ids_ref[k : k + 1, :] for k in range(4)]
    hots = [(ids[k] == expert).astype(jnp.float32) for k in range(4)]
    hot = (hots[0] + hots[1] + hots[2] + hots[3]).astype(jnp.bfloat16)
    sooner = lax.broadcasted_iota(jnp.int32, (count, count), 0)
    later = lax.broadcasted_iota(jnp.int32, (count, count), 1)
    before = jnp.dot(
        hot,
        ((later // 32 == sooner // 32) & (sooner < later)).astype(jnp.float32).astype(jnp.bfloat16),
        preferred_element_type=jnp.float32,
    )
    line = lax.broadcasted_iota(jnp.int32, (8, count), 0)
    offset = lax.broadcasted_iota(jnp.int32, (1, count), 1) // 32 % 4 * 8
    table = jnp.zeros((8, count), jnp.float32)
    for k in range(4):
        rank = jnp.sum(hots[k] * before, axis=0, keepdims=True)
        code = (ids[k] * 32 + offset).astype(jnp.float32) + rank
        table = jnp.where(line == k, code, table)
        table = jnp.where(line == 4 + k, gate_ref[k : k + 1, :], table)
    table_ref[...] = table

    members = lax.broadcasted_iota(jnp.int32, (8, count), 1)
    last = (((1,), (1,)), ((), ()))
    per_block = lax.dot_general(
        (members // 32 == line).astype(jnp.float32).astype(jnp.bfloat16),
        hot,
        last,
        preferred_element_type=jnp.float32,
    )
    place_of = lax.broadcasted_iota(jnp.int32, (8, 32), 0)
    per_owner = jnp.zeros((8, 32), jnp.float32)
    for block in range(8):
        owner = owners_ref[pl.ds(pick_ref[0, block], 1), :]
        per_owner = per_owner + jnp.where(place_of == owner, per_block[block : block + 1, :], 0.0)
    expert_row = lax.broadcasted_iota(jnp.int32, (32, 128), 0)
    owner_lane = lax.broadcasted_iota(jnp.int32, (32, 128), 1)
    own_line = lax.broadcasted_iota(jnp.int32, (8, 128), 0)
    own_lane = lax.broadcasted_iota(jnp.int32, (8, 128), 1)
    tallied = jnp.zeros((8, 128), jnp.float32)
    for j in range(2):
        moved = jnp.dot(
            per_owner.astype(jnp.bfloat16),
            (expert_row == owner_lane // 8 * 2 + j).astype(jnp.float32).astype(jnp.bfloat16),
            preferred_element_type=jnp.float32,
        )
        own = jnp.sum(jnp.where(own_lane % 8 == own_line, moved, 0.0), axis=0, keepdims=True)
        tallied = jnp.where(own_line == j, own, tallied)
    counts_ref[...] = tallied.astype(jnp.int32)

    for request in range(3):
        for group in range(KV_HEADS):
            values[request, group, :, HEAD_DIM:] = jnp.ones((CACHE, HEAD_DIM), jnp.bfloat16)
    for group in range(KV_HEADS):
        new_values[group, :, HEAD_DIM:] = jnp.ones((count, HEAD_DIM), jnp.bfloat16)

    wide = tokens_ref[...].astype(jnp.float32)
    scale = lax.rsqrt(jnp.mean(wide * wide, axis=1, keepdims=True) + epsilon)
    normed = (wide * scale * attn_gain_ref[...].reshape(1, -1)).astype(jnp.bfloat16)

    position = row + by_request(row, [cached[0], cached[1] - starts[1], cached[2] - starts[2]])
    angle = position.astype(jnp.float32) * inverse_ref[...]
    cosine = jnp.cos(angle)
    sine = jnp.sin(angle)
    sine = jnp.where(lane < HEAD_DIM // 2, -sine, sine)

    def turned(head):
        return (head * cosine + pltpu.roll(head, HEAD_DIM // 2, 1) * sine).astype(jnp.bfloat16)

    loads[0].wait()
    for part in range(HEADS // 2):
        pair = jnp.dot(
            normed,
            w_query[:, part * 256 : (part + 1) * 256],
            preferred_element_type=jnp.float32,
        )
        for side in range(2):
            queries[part * 2 + side] = turned(pair[:, side * HEAD_DIM : (side + 1) * HEAD_DIM])
    loads[1].wait()
    fresh_keys = jnp.dot(normed, w_key[...], preferred_element_type=jnp.float32)
    loads[2].wait()
    fresh_values = jnp.dot(normed, w_value[...], preferred_element_type=jnp.float32)
    for group in range(KV_HEADS):
        lanes = slice(group * HEAD_DIM, (group + 1) * HEAD_DIM)
        new_keys[group] = turned(fresh_keys[:, lanes])
        new_values[group, :, 0:HEAD_DIM] = fresh_values[:, lanes].astype(jnp.bfloat16)

    factor = HEAD_DIM ** (-0.5) * 1.4426950408889634
    stack = GROUP * TILE
    lowest = -jnp.inf
    for request in range(3):
        for copy in cache_loads(request):
            copy.wait()
        start, end, filled = starts[request], ends[request], cached[request]

        def attend(tile, carry, request=request, start=start, end=end, filled=filled):
            base = pl.multiple_of(tile * TILE, TILE)
            token = base + lax.broadcasted_iota(jnp.int32, (stack, 128), 0) % TILE
            here = filled + token - start
            slot = lax.broadcasted_iota(jnp.int32, (stack, 128), 1)
            near = (slot == 0) | (here - slot < CACHE)
            open_slot = OPEN + lax.broadcasted_iota(jnp.int32, (1, CACHE - OPEN), 1)
            bias = jnp.where(open_slot < filled, 0.0, lowest)
            fresh = lax.broadcasted_iota(jnp.int32, (stack, count), 1)
            asking = base + lax.broadcasted_iota(jnp.int32, (stack, count), 0) % TILE
            seen = (fresh >= start) & (fresh <= asking)
            inside = (token >= start) & (token < end)
            for group in range(KV_HEADS):
                asked = queries[group * GROUP : (group + 1) * GROUP, pl.ds(base, TILE), :].reshape(
                    stack, HEAD_DIM
                )

                def score(block):
                    return lax.dot_general(asked, block, last, preferred_element_type=jnp.float32)

                parts = [
                    jnp.where(near, score(keys[request, group, 0:128, :]), lowest),
                    score(keys[request, group, 128:OPEN, :]),
                    score(keys[request, group, OPEN:CACHE, :]) + bias,
                    jnp.where(seen, score(new_keys[group]), lowest),
                ]
                peak = jnp.max(parts[0], axis=1, keepdims=True)
                for part in parts[1:]:
                    peak = jnp.maximum(peak, jnp.max(part, axis=1, keepdims=True))
                peak = peak * factor
                blocks = [
                    values[request, group, 0:128, :],
                    values[request, group, 128:OPEN, :],
                    values[request, group, OPEN:CACHE, :],
                    new_values[group],
                ]
                mixed = jnp.zeros((stack, 2 * HEAD_DIM), jnp.float32)
                for part, block in zip(parts, blocks):
                    weight = jnp.exp2(part * factor - peak).astype(jnp.bfloat16)
                    mixed = mixed + jnp.dot(weight, block, preferred_element_type=jnp.float32)
                answer = mixed[:, 0:HEAD_DIM] / mixed[:, HEAD_DIM:]
                for member in range(GROUP):
                    rows = slice(member * TILE, (member + 1) * TILE)
                    head = group * GROUP + member
                    spot = (pl.ds(base, TILE), slice(head * HEAD_DIM, (head + 1) * HEAD_DIM))
                    kept = attended[spot].astype(jnp.float32)
                    attended[spot] = jnp.where(inside[rows], answer[rows], kept).astype(jnp.bfloat16)
            return carry

        lax.fori_loop(start // TILE, (end + TILE - 1) // TILE, attend, 0)

    last_load.wait()
    projected = jnp.dot(attended[...], w_out[...], preferred_element_type=jnp.float32)
    residual = (tokens_ref[...].astype(jnp.float32) + projected).astype(jnp.bfloat16)
    residual_ref[...] = residual
    wide = residual.astype(jnp.float32)
    scale = lax.rsqrt(jnp.mean(wide * wide, axis=1, keepdims=True) + epsilon)
    normed_ref[...] = (wide * scale * ffn_gain_ref[...].reshape(1, -1)).astype(jnp.bfloat16)


def front(
    tokens,
    attn_gain,
    ffn_gain,
    w_query,
    w_key,
    w_value,
    w_out,
    key_cache,
    value_cache,
    lengths,
    cached,
    pick,
    ids,
    gates,
    replica_owner,
):
    count, width = tokens.shape
    any_space = pl.BlockSpec(memory_space=pl.ANY)
    vmem = pl.BlockSpec(memory_space=pltpu.VMEM)
    smem = pl.BlockSpec(memory_space=pltpu.SMEM)
    dma = pltpu.SemaphoreType.DMA
    bf16 = jnp.bfloat16
    rates = np.float32(rope_base) ** (-(np.arange(HEAD_DIM // 2, dtype=np.float32) * 2.0 / HEAD_DIM))
    inverse = jnp.asarray(np.concatenate([rates, rates])[None, :].astype(np.float32))
    return pl.pallas_call(
        front_kernel,
        out_shape=(
            jax.ShapeDtypeStruct((count, width), bf16),
            jax.ShapeDtypeStruct((count, width), bf16),
            jax.ShapeDtypeStruct((8, count), jnp.float32),
            jax.ShapeDtypeStruct((8, 128), jnp.int32),
        ),
        in_specs=[smem] * 3 + [vmem] * 7 + [any_space] * 6,
        out_specs=(vmem,) * 4,
        scratch_shapes=[
            pltpu.VMEM(w_query.shape, bf16),
            pltpu.VMEM(w_key.shape, bf16),
            pltpu.VMEM(w_value.shape, bf16),
            pltpu.VMEM(w_out.shape, bf16),
            pltpu.VMEM((3, KV_HEADS, CACHE, HEAD_DIM), bf16),
            pltpu.VMEM((3, KV_HEADS, CACHE, 2 * HEAD_DIM), bf16),
            pltpu.VMEM((KV_HEADS, count, HEAD_DIM), bf16),
            pltpu.VMEM((KV_HEADS, count, 2 * HEAD_DIM), bf16),
            pltpu.VMEM((HEADS, count, HEAD_DIM), bf16),
            pltpu.VMEM((count, HEADS * HEAD_DIM), bf16),
            dma((4,)),
            dma((3, KV_HEADS)),
            dma((3, KV_HEADS)),
        ],
        name="front",
        compiler_params=pltpu.CompilerParams(vmem_limit_bytes=58 << 20),
        cost_estimate=pl.CostEstimate(flops=12 * 10**9, bytes_accessed=60 * 10**6, transcendentals=10**7),
    )(
        lengths,
        cached,
        pick,
        tokens,
        attn_gain,
        ffn_gain,
        inverse,
        ids.T,
        gates.T,
        replica_owner.T,
        w_query,
        w_key,
        w_value,
        w_out,
        key_cache,
        value_cache,
    )


MESH = pl.DeviceIdType.MESH
SIDE = 4
SLOTS = 32
HALF = 128
WIDTH = 1536
HIDDEN = 768
CHUNK = 2 * SIDE * SLOTS
PARTNERS = [
    (dz, dx, dy, dc)
    for dz in range(SIDE)
    for dx in range(SIDE)
    for dy in range(SIDE)
    for dc in range(2)
    if (dz == 0) + (dx == 0) + (dy == 0) >= 2 and (dz, dx, dy, dc) != (0, 0, 0, 0)
]


def place():
    row, column = lax.axis_index("dp"), lax.axis_index("expert")
    return row // SIDE, row % SIDE, column // 2, column % 2


def device_at(dz, dx, dy, dc):
    z, x, y, c = place()
    row = ((z + dz) % SIDE) * SIDE + (x + dx) % SIDE
    return (row, ((y + dy) % SIDE) * 2 + (c + dc) % 2)


def along(half, offset, dc=0):
    return device_at(half * offset, (1 - half) * offset, 0, dc)


def across(half, offset):
    return device_at((1 - half) * offset, half * offset, 0, 0)


def send(source, landing, sem_s, sem_r, device):
    return pltpu.make_async_remote_copy(
        src_ref=source,
        dst_ref=landing,
        send_sem=sem_s,
        recv_sem=sem_r,
        device_id=device,
        device_id_type=MESH,
    )


def moe_kernel(
    rows_ref,
    table_ref,
    counts_ref,
    residual_ref,
    gate_up_ref,
    down_a,
    down_b,
    down_c,
    down_d,
    out_ref,
    owner_ref,
    held,
    tables,
    packed,
    landed,
    done,
    back_rows,
    partial,
    given,
    total,
    gate_up,
    down,
    tallies,
    told,
    s_first,
    r_first,
    s_table,
    r_table,
    s_out,
    r_out,
    s_back,
    r_back,
    s_give,
    r_give,
    s_tally,
    r_tally,
    s_weight,
    r_weight,
    s_pass,
    r_pass,
    d_down,
    s_down,
    r_down,
    s_relay,
    r_relay,
    lent,
    s_lend,
    r_lend,
):
    down_refs = (down_a, down_b, down_c, down_d)
    z, x, y, c = place()
    barrier = pltpu.get_barrier_semaphore()
    for offsets in PARTNERS:
        pl.semaphore_signal(barrier, inc=1, device_id=device_at(*offsets), device_id_type=MESH)
    pl.semaphore_wait(barrier, len(PARTNERS))

    first = []
    for back in (1, 3, 2):
        for half in range(2):
            there = across(half, back)
            first.append(
                send(table_ref, tables.at[half, back], s_table.at[half, back], r_table.at[half, back], there)
            )
            if back != 2:
                first.append(
                    send(
                        rows_ref.at[pl.ds(half * HALF, HALF)],
                        held.at[half, back],
                        s_first.at[half, back],
                        r_first.at[half, back],
                        there,
                    )
                )
    for copy in first:
        copy.start()

    column = y * 2 + c
    shards = {}
    for dc in range(2):
        expert = (c + dc) % 2
        for dy in (1, 3, 0):
            source, landing = gate_up_ref.at[expert], gate_up.at[:, column]
            if dy == 0 and dc == 0:
                own_shard = pltpu.make_async_copy(source, landing, r_weight.at[dy, dc])
                own_shard.start()
            else:
                shards[dy, dc] = send(
                    source, landing, s_weight.at[dy, dc], r_weight.at[dy, dc], device_at(0, 0, dy, dc)
                )
                shards[dy, dc].start()
    near_down, far_down = [], []
    for back, shard in enumerate(down_refs):
        spot = down.at[((y + SIDE - back) % SIDE) * 2 + c]
        near_down.append(pltpu.make_async_copy(shard.at[c], spot, d_down.at[back]))
        far_down.append(
            send(shard.at[1 - c], spot, s_down.at[back], r_down.at[back], device_at(0, 0, 0, 1))
        )
    for copy in near_down + far_down:
        copy.start()

    tallies[0] = counts_ref[...]
    legs = [
        [(0, 1, 0, 0), (0, 2, 0, 0), (0, 3, 0, 0)],
        [(1, 0, 0, 0), (2, 0, 0, 0), (3, 0, 0, 0)],
        [(0, 0, 1, 0), (0, 0, 2, 0), (0, 0, 3, 0)],
        [(0, 0, 0, 1)],
    ]

    def tally(leg):
        copies = [
            send(tallies.at[leg], told.at[leg, k], s_tally.at[leg, k], r_tally.at[leg, k], device_at(*offsets))
            for k, offsets in enumerate(legs[leg])
        ]
        for copy in copies:
            copy.start()
        return copies

    def add_tallies(leg, copies):
        held_so_far = tallies[leg]
        for k, copy in enumerate(copies):
            copy.wait()
            held_so_far = held_so_far + told[leg, k]
        return held_so_far

    telling = tally(0)

    held[0, 0] = rows_ref[0:HALF, :]
    held[1, 0] = rows_ref[HALF : 2 * HALF, :]
    tables[0, 0] = table_ref[...]
    tables[1, 0] = table_ref[...]
    line = lax.broadcasted_iota(jnp.int32, (CHUNK, HALF), 0)

    def copies_out(half, back):
        at = (1 - half) * x + half * z
        copies = []
        for dc in (1, 0):
            for offset in (2, 1, 3, 0):
                piece = packed.at[half, back, (at + offset) % SIDE, (c + dc) % 2]
                landing = landed.at[half, back, offset, dc]
                arrival = r_out.at[half, back, offset, dc]
                if offset == 0 and dc == 0:
                    copies.append(pltpu.make_async_copy(piece, landing, arrival))
                else:
                    copies.append(
                        send(piece, landing, s_out.at[half, back, offset, dc], arrival, along(half, offset, dc))
                    )
        return copies

    def pack(half, back):
        if half == 0:
            wanted = line + z * CHUNK
        else:
            wanted = (line // 64) * CHUNK + x * 64 + line % 64
        table = tables[half, back]
        hot = jnp.zeros((CHUNK, HALF), jnp.bool_)
        for k in range(4):
            code = table[k : k + 1, half * HALF : (half + 1) * HALF].astype(jnp.int32)
            hot = hot | (code == wanted)
        spread = jnp.dot(
            hot.astype(jnp.float32).astype(jnp.bfloat16),
            held[half, back],
            preferred_element_type=jnp.float32,
        ).astype(jnp.bfloat16)
        packed[half, back] = spread.reshape(SIDE, 2, SLOTS, WIDTH)
        for copy in copies_out(half, back):
            copy.start()

    def relay(half, side):
        rows = pl.ds(side * (HALF // 2), HALF // 2)
        return send(
            held.at[half, 1 + 2 * side, rows],
            held.at[half, 2, rows],
            s_relay.at[half, side],
            r_relay.at[half, side],
            across(half, 1 + 2 * side),
        )

    def arrive(half, back):
        send(
            table_ref,
            tables.at[half, back],
            s_table.at[half, back],
            r_table.at[half, back],
            across(half, back),
        ).wait_recv()
        if back == 2:
            for side in range(2):
                relay(half, side).wait_recv()
        else:
            send(
                rows_ref.at[pl.ds(half * HALF, HALF)],
                held.at[half, back],
                s_first.at[half, back],
                r_first.at[half, back],
                across(half, back),
            ).wait_recv()
            relay(half, back // 2).start()

    for half in range(2):
        pack(half, 0)
    for back in (1, 3, 2):
        for half in range(2):
            arrive(half, back)
        for half in range(2):
            pack(half, back)

    passing = []
    for dc in range(2):
        for side, (dy, onward, low) in enumerate(((1, 1, 0), (3, 3, 1))):
            owner = ((y + SIDE - dy) % SIDE) * 2 + (c + dc) % 2
            whole = gate_up.at[:, owner]
            piece = gate_up.at[:, owner, pl.ds(low * 48, 48)]
            send(whole, whole, s_weight.at[dy, dc], r_weight.at[dy, dc], device_at(0, 0, dy, dc)).wait_recv()
            copy = send(
                piece, piece, s_pass.at[side, dc], r_pass.at[side, dc], device_at(0, 0, onward, 0)
            )
            copy.start()
            passing.append(copy)

    tallies[1] = add_tallies(0, telling)
    telling = tally(1)

    for copy in near_down:
        copy.wait()
    for copy in far_down:
        copy.wait_recv()
    own_shard.wait()
    shards[0, 1].wait_recv()
    for copy in passing:
        copy.wait()

    def copies_back(half, back, own=True):
        copies = []
        for dc in (1, 0):
            for offset in (2, 1, 3, 0):
                if offset == 0 and dc == 0 and not own:
                    continue
                piece = done.at[half, back, offset, dc]
                landing = back_rows.at[half, back, offset, dc]
                arrival = r_back.at[half, back, offset, dc]
                if offset == 0 and dc == 0:
                    copies.append((pltpu.make_async_copy(piece, landing, arrival), False))
                else:
                    copies.append(
                        (
                            send(
                                piece,
                                landing,
                                s_back.at[half, back, offset, dc],
                                arrival,
                                along(half, SIDE - offset, dc),
                            ),
                            True,
                        )
                    )
        return copies

    last = (((1,), (1,)), ((), ()))

    def serve(step, carry):
        half, back = step % 2, step // 2
        for copy in copies_out(half, back):
            copy.wait()
        arrived = landed[half, back].reshape(CHUNK, WIDTH)
        gate = lax.dot_general(
            arrived, gate_up[0].reshape(HIDDEN, WIDTH), last, preferred_element_type=jnp.float32
        )
        up = lax.dot_general(
            arrived, gate_up[1].reshape(HIDDEN, WIDTH), last, preferred_element_type=jnp.float32
        )
        hidden = (jnp.maximum(gate, 0.0) * up).astype(jnp.bfloat16)
        answer = lax.dot_general(
            hidden, down[...].reshape(WIDTH, HIDDEN), last, preferred_element_type=jnp.float32
        )
        done[half, back] = answer.astype(jnp.bfloat16).reshape(SIDE, 2, SLOTS, WIDTH)
        for copy, _ in copies_back(half, back):
            copy.start()
        return carry

    lax.fori_loop(0, 2 * SIDE, serve, 0)
    tallies[2] = add_tallies(1, telling)
    telling = tally(2)

    turn, swap, slot = line // 64, (line // 32) % 2, line % 32

    def mix(half, back):
        for copy, remote in copies_back(half, back):
            if remote:
                copy.wait_recv()
            else:
                copy.wait()
        if half == 0:
            owner = z * SIDE + (x + turn) % SIDE
        else:
            owner = ((z + turn) % SIDE) * SIDE + x
        wanted = owner * 64 + ((c + swap) % 2) * 32 + slot
        table = tables[half, back]
        weight = jnp.zeros((CHUNK, HALF), jnp.float32)
        for k in range(4):
            code = table[k : k + 1, half * HALF : (half + 1) * HALF].astype(jnp.int32)
            gate = table[4 + k : 5 + k, half * HALF : (half + 1) * HALF]
            weight = weight + jnp.where(code == wanted, gate, 0.0)
        coarse = weight.astype(jnp.bfloat16)
        fine = (weight - coarse.astype(jnp.float32)).astype(jnp.bfloat16)
        came = back_rows[half, back].reshape(CHUNK, WIDTH)
        rows = (((0,), (0,)), ((), ()))
        return lax.dot_general(
            coarse, came, rows, preferred_element_type=jnp.float32
        ) + lax.dot_general(fine, came, rows, preferred_element_type=jnp.float32)

    def gift(half, back):
        return send(
            partial.at[half, back],
            given.at[half, back],
            s_give.at[half, back],
            r_give.at[half, back],
            across(half, SIDE - back),
        )

    def lend(half, side):
        rows = pl.ds(side * (HALF // 2), HALF // 2)
        return send(
            partial.at[half, 2, rows],
            lent.at[half, side],
            s_lend.at[half, side],
            r_lend.at[half, side],
            across(half, 3 - 2 * side),
        )

    for half in range(2):
        partial[half, 2] = mix(half, 2).astype(jnp.bfloat16)
        for side in range(2):
            lend(half, side).start()
    for side in range(2):
        back = 1 + 2 * side
        for half in range(2):
            share = mix(half, back)
            lend(half, side).wait_recv()
            rows = slice(side * (HALF // 2), (side + 1) * (HALF // 2))
            others = slice((1 - side) * (HALF // 2), (2 - side) * (HALF // 2))
            partial[half, back, rows] = (share[rows] + lent[half, side].astype(jnp.float32)).astype(jnp.bfloat16)
            partial[half, back, others] = share[others].astype(jnp.bfloat16)
            gift(half, back).start()
    tallies[3] = add_tallies(2, telling)
    telling = tally(3)
    for half in range(2):
        total[half] = mix(half, 0)
    tallied = add_tallies(3, telling)
    me = lax.axis_index("dp") * 8 + lax.axis_index("expert")
    lane = lax.broadcasted_iota(jnp.int32, tallied.shape, 1)
    mine = jnp.sum(jnp.where(lane == me, tallied, 0).astype(jnp.float32), axis=1, keepdims=True)
    line_of = lax.broadcasted_iota(jnp.int32, tallied.shape, 0)
    owned = jnp.sum(jnp.where(line_of == lane, mine, 0.0), axis=0, keepdims=True)
    owner_ref[...] = owned[:, 0:2].astype(jnp.int32)
    for half in range(2):
        mixed = total[half]
        for back in (1, 3):
            gift(half, back).wait_recv()
            mixed = mixed + given[half, back].astype(jnp.float32)
        here = pl.ds(half * HALF, HALF)
        out_ref[here, :] = (residual_ref[here, :].astype(jnp.float32) + mixed).astype(jnp.bfloat16)

    for copy in first:
        copy.wait_send()
    for half in range(2):
        for side in range(2):
            relay(half, side).wait_send()
    for copy in list(shards.values()) + far_down:
        copy.wait_send()

    def settle(step, carry):
        half, back = step % 2, step // 2
        for copy, _ in copies_back(half, back, own=False):
            copy.wait_send()
        return carry

    lax.fori_loop(0, 2 * SIDE, settle, 0)
    for half in range(2):
        for back in (1, 3):
            gift(half, back).wait_send()
        for side in range(2):
            lend(half, side).wait_send()


def moe(rows, table, counts, residual, gate_up, downs):
    any_space = pl.BlockSpec(memory_space=pl.ANY)
    vmem = pl.BlockSpec(memory_space=pltpu.VMEM)
    dma = pltpu.SemaphoreType.DMA
    chunks = (2, SIDE, SIDE, 2, SLOTS, WIDTH)
    halves = (2, SIDE, HALF, WIDTH)
    bf16 = jnp.bfloat16
    return pl.pallas_call(
        moe_kernel,
        out_shape=(
            jax.ShapeDtypeStruct((2 * HALF, WIDTH), bf16),
            jax.ShapeDtypeStruct((1, 2), jnp.int32),
        ),
        in_specs=[vmem] * 4 + [any_space] * 5,
        out_specs=(vmem, vmem),
        scratch_shapes=[
            pltpu.VMEM(halves, bf16),
            pltpu.VMEM((2, SIDE, 8, 2 * HALF), jnp.float32),
            pltpu.VMEM(chunks, bf16),
            pltpu.VMEM(chunks, bf16),
            pltpu.VMEM(chunks, bf16),
            pltpu.VMEM(chunks, bf16),
            pltpu.VMEM(halves, bf16),
            pltpu.VMEM(halves, bf16),
            pltpu.VMEM((2, HALF, WIDTH), jnp.float32),
            pltpu.VMEM((2, 8, 96, WIDTH), bf16),
            pltpu.VMEM((8, 192, HIDDEN), bf16),
            pltpu.VMEM((4, 8, 128), jnp.int32),
            pltpu.VMEM((4, 3, 8, 128), jnp.int32),
            dma((2, SIDE)),
            dma((2, SIDE)),
            dma((2, SIDE)),
            dma((2, SIDE)),
            dma((2, SIDE, SIDE, 2)),
            dma((2, SIDE, SIDE, 2)),
            dma((2, SIDE, SIDE, 2)),
            dma((2, SIDE, SIDE, 2)),
            dma((2, SIDE)),
            dma((2, SIDE)),
            dma((4, 3)),
            dma((4, 3)),
            dma((SIDE, 2)),
            dma((SIDE, 2)),
            dma((2, 2)),
            dma((2, 2)),
            dma((SIDE,)),
            dma((SIDE,)),
            dma((SIDE,)),
            dma((2, 2)),
            dma((2, 2)),
            pltpu.VMEM((2, 2, HALF // 2, WIDTH), bf16),
            dma((2, 2)),
            dma((2, 2)),
        ],
        name="moe",
        compiler_params=pltpu.CompilerParams(
            collective_id=1, has_side_effects=True, vmem_limit_bytes=60 << 20
        ),
        cost_estimate=pl.CostEstimate(flops=17 * 10**9, bytes_accessed=10**7, transcendentals=0),
    )(rows, table, counts, residual, gate_up, *downs)


def on_device(
    tokens,
    attn_gain,
    ffn_gain,
    w_query,
    w_key,
    w_value,
    w_out,
    key_cache,
    value_cache,
    req_lengths,
    cache_lengths,
    expert_ids,
    route_gate,
    replica_owner,
    replica_pick,
    w_gate_up,
    w_down,
):
    columns = lax.axis_size("expert")
    downs = [w_down] + [
        lax.ppermute(w_down, "expert", [(i, (i + 2 * k) % columns) for i in range(columns)])
        for k in range(1, columns // 2)
    ]
    residual, normed_mid, table, counts = front(
        tokens,
        attn_gain,
        ffn_gain,
        w_query,
        w_key,
        w_value,
        w_out,
        key_cache,
        value_cache,
        req_lengths,
        cache_lengths,
        replica_pick,
        expert_ids,
        route_gate,
        replica_owner,
    )
    return moe(
        normed_mid, table, counts, residual, w_gate_up.transpose(0, 2, 1, 3), downs
    )


def solution(mesh):
    in_specs = (
        P(("dp", "expert"), None),
        P(),
        P(),
        P(),
        P(),
        P(),
        P(),
        P(("dp", "expert"), None, None),
        P(("dp", "expert"), None, None),
        P(("dp", "expert"), None),
        P(("dp", "expert"), None),
        P(("dp", "expert"), None),
        P(("dp", "expert"), None),
        P(),
        P(("dp", "expert"), None),
        P("dp", "expert", None, None),
        P("dp", "expert", None),
    )
    out_specs = (P(("dp", "expert"), None), P(("dp", "expert"), None))
    return jax.shard_map(
        on_device, mesh=mesh, in_specs=in_specs, out_specs=out_specs, check_vma=False
    )
```
